32 devices in a mesh: groups: 2 (over x), blocks: 16 (over z, y, core).
Axes of the slice: x: 2, y: 2, z: 4, core: 2. Of those that a mesh axis runs over, the one named last changes fastest.
Arguments:
- estimate: float32 [512, 128, 128], P(('groups', 'blocks')), parts along dimension 0, may hold values from 0.5 to 1.5
- images: bfloat16 [8, 512, 128, 128], P(None, ('groups', 'blocks')), parts along dimension 1, may hold values from 0.25 to 2
- point_spread: float32 [8, 3, 31], replicated, may hold values from 0.05 to 1
- shifts: int32 [8], replicated, may hold values from -32 to 32, as said below
Outputs:
- restored: float32 [512, 128, 128], P(('groups', 'blocks')), parts along dimension 0
The draws below stay inside these ranges and needn't reach their ends.
There are 2 independent parts, one for each index of `groups`. The reference program is written for one: setup_inputs(seed, part) draws one part's arguments, and reference() takes and returns one part's arrays. A program takes and returns all parts, laid end to end along the dimension named above; an argument that names none is the same for every part. Nothing has to cross between parts.
Inputs may be any that keep to these rules, and one draw needn't show every extreme that they name: `shifts`: one view is placed at exactly 32 and another at exactly -32.
All inputs are finite; a program needn't handle non-finite values.
Results may differ from the reference program's by a relative error of at most 0.00031.
Values may be sent and summed in bfloat16 or wider, within the bound.
A program may use at most 128 MiB of HBM per device.

```python
import math
import jax
import jax.numpy as jnp
from jax import lax

VIEWS = 8
TAPS = 31
NY = 128
NZ = 128
ITERS = 1
SLAB = 256
SHIFT = 32


def draw_shifts(key, part):
    first_key, second_key = jax.random.split(key)
    values = jax.random.randint(first_key, (VIEWS,), 0 - SHIFT, SHIFT + 1)
    order = jax.random.permutation(second_key, VIEWS)
    values = values.at[order[0]].set(SHIFT)
    values = values.at[order[1]].set(0 - SHIFT)
    return values.astype(jnp.int32)


def block_scale(own_key, shape, pieces, smallest, top_value):
    def one(dim, parts):
        steps = jax.random.uniform(jax.random.fold_in(jax.random.fold_in(own_key, 6), dim), (parts,), jnp.float32, smallest / len(pieces), top_value / len(pieces))
        return jnp.repeat(jnp.exp(steps), shape[dim] // parts).reshape((-1,) + (1,) * (len(shape) - dim - 1))

    level = one(*pieces[0])
    for cut in pieces[1:]:
        level = level * one(*cut)
    return level


def setup_inputs(seed: int = 0, part: int = 0) -> dict:
    key_of = jax.random.split(jax.random.key(seed), 5)
    own_keys = jax.random.split(jax.random.fold_in(key_of[4], part), 5)
    return {
        "estimate": jnp.clip(0.5 + 1.0 * jax.random.uniform(own_keys[0], (SLAB, NY, NZ), jnp.float32) ** block_scale(own_keys[0], (SLAB, NY, NZ), ((0, 16),), -0.2, 0.2), 0.5, 1.5),
        "images": jnp.clip(0.25 + 1.75 * jax.random.uniform(own_keys[1], (VIEWS, SLAB, NY, NZ), jnp.float32) ** block_scale(own_keys[1], (VIEWS, SLAB, NY, NZ), ((1, 16),), -0.2, 0.2), 0.25, 2.0).astype(jnp.bfloat16),
        "point_spread": jnp.clip(jnp.exp(jax.random.uniform(key_of[2], (VIEWS, 3, TAPS), jnp.float32, math.log(0.05), math.log(1.0))), 0.05, 1.0),
        "shifts": draw_shifts(jax.random.fold_in(key_of[4], 71), part),
    }


def banded(tap_values, count_in, count_out, offset, direction):
    row_index = jnp.arange(count_in)[:, None]
    col_index = jnp.arange(count_out)[None, :]
    position = direction * (row_index - col_index) + offset
    matches = position[:, :, None] == jnp.arange(tap_values.shape[0])[None, None, :]
    spread = jnp.where(matches, tap_values.astype(jnp.float32)[None, None, :], jnp.float32(0.0))
    return jnp.sum(spread, axis=2).astype(jnp.bfloat16)


def forward_x(blurred, tap_values):
    margin = tap_values.shape[0] // 2
    slab_rows = blurred.shape[0]
    padded = jnp.pad(blurred.astype(jnp.float32), ((margin, margin), (0, 0), (0, 0)))
    summed = jnp.zeros(blurred.shape, jnp.float32)
    for tap in range(tap_values.shape[0]):
        summed = summed + tap_values[tap].astype(jnp.float32) * padded[tap:tap + slab_rows]
    return summed


def adjoint_x(quotient, tap_values):
    margin = tap_values.shape[0] // 2
    slab_rows = quotient.shape[0]
    padded = jnp.pad(quotient.astype(jnp.float32), ((margin, margin), (0, 0), (0, 0)))
    summed = jnp.zeros(quotient.shape, jnp.float32)
    for tap in range(tap_values.shape[0]):
        start = 2 * margin - tap
        summed = summed + tap_values[tap].astype(jnp.float32) * padded[start:start + slab_rows]
    return summed


def reference(estimate, images, point_spread, shifts):
    kernel = (point_spread / jnp.sum(point_spread, axis=2, keepdims=True)).astype(jnp.bfloat16)
    slab_rows = estimate.shape[0]
    padded = jnp.pad(images, ((0, 0), (SHIFT, SHIFT), (0, 0), (0, 0)))
    aligned = []
    for view in range(VIEWS):
        start = (SHIFT + shifts[view]).astype(jnp.int32)
        aligned.append(lax.dynamic_slice_in_dim(padded[view], start, slab_rows, 0))
    current = estimate
    for sweep in range(ITERS):
        current_b = current.astype(jnp.bfloat16)
        summed = jnp.zeros(estimate.shape, jnp.float32)
        for view in range(VIEWS):
            z_matrix = banded(kernel[view, 2], NZ, NZ, 15, 1)
            y_matrix = banded(kernel[view, 1], NY, NY, 15, 1)
            blur_z = jnp.dot(current_b.reshape(-1, NZ), z_matrix, preferred_element_type=jnp.float32)
            blur_z = blur_z.astype(jnp.bfloat16).reshape(slab_rows, NY, NZ)
            blur_y = jnp.einsum('xyz,yk->xkz', blur_z.astype(jnp.float32), y_matrix.astype(jnp.float32)).astype(jnp.bfloat16)
            predicted = forward_x(blur_y, kernel[view, 0])
            quotient = (aligned[view].astype(jnp.float32) / predicted).astype(jnp.bfloat16)
            back_x = adjoint_x(quotient, kernel[view, 0]).astype(jnp.bfloat16)
            back_y = jnp.einsum('xkz,yk->xyz', back_x.astype(jnp.float32), y_matrix.astype(jnp.float32)).astype(jnp.bfloat16)
            correction = jnp.dot(back_y.reshape(-1, NZ), z_matrix.T, preferred_element_type=jnp.float32)
            summed = summed + correction.reshape(slab_rows, NY, NZ)
        current = current * summed / VIEWS
    return current
```

```python
import functools

import jax
import jax.numpy as jnp
from jax import lax
from jax.experimental import pallas as pl
from jax.experimental.pallas import tpu as pltpu
from jax.sharding import PartitionSpec as P

SHIFT = 32
PARTS = 8
TOP = 4.2
F32 = jnp.float32
BF16 = jnp.bfloat16
I16 = jnp.int16
I32 = jnp.int32
MESH = pl.DeviceIdType.MESH


def dot(a, b):
    return jnp.dot(a, b, preferred_element_type=F32)


def coded(x):
    return ((x + 0.5).astype(I32) - 32768).astype(I16)


def decoded(q):
    return (q.astype(I32) + 32768).astype(F32)


def fused_kernel(
    dims,
    est_hbm,
    img_hbm,
    spread_ref,
    shift_ref,
    out_ref,
    est,
    img,
    win,
    held,
    own,
    mate_out,
    mate_in,
    far_out,
    far_in,
    on_out,
    on_in,
    dir_out,
    dir_in,
    taps,
    x_tmp,
    x_fwd,
    x_adj,
    z_fwd,
    z_adj,
    y_fwd,
    y_adj,
    scale,
    unscale,
    local_sem,
    send_sem,
    recv_sem,
    back_send,
    back_recv,
):
    count, views, rows, across, along, tap_count, hops = dims
    margin = tap_count // 2
    part = across // PARTS
    mid = hops
    slab = rows * count
    me = lax.axis_index("blocks")
    odd = lax.rem(me, 2)
    right = lax.rem(me, 4) // 2
    mate = 1 - 2 * odd
    far = -3 * mate
    side = 2 - 4 * right
    up = 2 - 2 * right
    down = 2 * right
    beyond = (me + 2 * side >= 0) & (me + 2 * side < count)
    before = (me - 2 * side >= 0) & (me - 2 * side < count)
    away = (me + far >= 0) & (me + far < count)

    barrier = pltpu.get_barrier_semaphore()

    def signal(there):
        pl.semaphore_signal(barrier, inc=1, device_id={"blocks": there}, device_id_type=MESH)

    signal(me + mate)
    signal(me + side)
    pl.when(beyond)(lambda: signal(me + 2 * side))
    pl.when(before)(lambda: signal(me - 2 * side))
    pl.when(away)(lambda: signal(me + far))

    def span(j):
        return pl.ds(pl.multiple_of(j * part, part), part)

    def load_est(j):
        return pltpu.make_async_copy(est_hbm.at[:, span(j)], est.at[:, span(j)], local_sem.at[j])

    load_img = pltpu.make_async_copy(img_hbm, img, local_sem.at[PARTS])

    @pl.loop(0, PARTS)
    def _(j):
        load_est(j).start()

    load_img.start()

    def send(from_slot, to_slot, there, kind, j):
        return pltpu.make_async_remote_copy(
            src_ref=win.at[from_slot, span(j)],
            dst_ref=win.at[to_slot, span(j)],
            send_sem=send_sem.at[kind, j],
            recv_sem=recv_sem.at[to_slot, j],
            device_id={"blocks": there},
            device_id_type=MESH,
        )

    def direct(j):
        return send(mid, mid - side, me + side, 0, j)

    def onward(j):
        return send(mid + side, mid - side, me + 2 * side, 1, j)

    def long(j):
        return send(mid, mid - far, me + far, 2, j)

    def near(j):
        return send(mid, mid - mate, me + mate, 3, j)

    def pass_near(j):
        return send(mid + side, mid + side - mate, me + mate, 4, j)

    def pass_back(j):
        return send(mid - side, mid - side - mate, me + mate, 5, j)

    def landed(offset, j):
        return send(mid, mid + offset, me + mate, 0, j)

    @pl.loop(0, PARTS)
    def _(j):
        load_est(j).wait()
        win[mid, span(j)] = jnp.swapaxes(est[:, span(j), :].astype(BF16), 0, 1)

    peers = 2 + beyond.astype(I32) + before.astype(I32) + away.astype(I32)
    pl.semaphore_wait(barrier, peers)

    @pl.loop(0, PARTS)
    def _(j):
        direct(j).start()
        pl.when(away)(lambda: long(j).start())
        near(j).start()

    for offset in range(-hops, hops + 1):
        there = me + offset
        if offset:

            @pl.when((there < 0) | (there >= count))
            def _():
                win[mid + offset] = jnp.zeros(win.shape[1:], BF16)

    def none_in(ref):
        ref[...] = jnp.full(ref.shape, -32768, I16)

    pl.when(jnp.logical_not(beyond))(lambda: none_in(on_in))
    pl.when(jnp.logical_not(away))(lambda: none_in(far_in))

    taps[...] = jnp.zeros(taps.shape, F32)
    for v in range(views):
        for a in range(3):
            line = spread_ref[v, pl.ds(a, 1), :]
            total = jnp.sum(line, axis=1, keepdims=True)
            taps[pl.ds(a * views + v, 1), pl.ds(0, tap_count)] = (line / total).astype(BF16).astype(F32)
    every = taps[...].astype(BF16)
    r = lax.broadcasted_iota(I32, (along, along), 0)
    c = lax.broadcasted_iota(I32, (along, along), 1)
    place = jnp.where(c < along // 2, c, c - along)
    plus = dot(every, (r == margin + place).astype(F32).astype(BF16))
    minus = dot(every, (r == margin - place).astype(F32).astype(BF16))
    close = jnp.abs(r - c) <= margin

    def turned(lines, row):
        line = jnp.broadcast_to(lines[row : row + 1], (along, along))
        return jnp.where(close, pltpu.roll(line, 0, 1, stride=1, stride_axis=0), 0.0)

    z_fwd[...] = jnp.zeros(z_fwd.shape, BF16)
    z_adj[...] = jnp.zeros(z_adj.shape, BF16)
    gains = [[], [], []]
    for v in range(views):
        half = pl.ds((v % 2) * along, along)
        for a in range(3):
            m = turned(minus, a * views + v)
            p = turned(plus, a * views + v).astype(BF16)
            inv = 1.0 / jnp.sum(m, axis=0, keepdims=True)
            gains[a].append(dot(jnp.broadcast_to(inv, (16, along)).astype(BF16), p)[:1])
            if a == 1:
                y_fwd[v] = p
                y_adj[v] = m.astype(BF16)
            if a == 2:
                z_fwd[v // 2, half, half] = m.astype(BF16)
                z_adj[v // 2, half, half] = p
    gain_x, gain_y, gain_z = [jnp.concatenate(g, axis=0) for g in gains]
    left = gain_y * jnp.max(gain_x, axis=1, keepdims=True)
    bound = lax.dot_general(left, gain_z, (((0,), (0,)), ((), ())), preferred_element_type=F32)
    bound = bound * (TOP * 1.03)
    scale[...] = 65535.0 / bound
    unscale[...] = bound / (65535.0 * views)

    shifts = jnp.zeros((views, along), I32)
    v_of = lax.broadcasted_iota(I32, (views, along), 0)
    w_of = lax.broadcasted_iota(I32, (views, along), 1)
    for v in range(views):
        shifts = jnp.where(v_of == v, shift_ref[v], shifts)
    index = w_of + shifts + (margin - rows * hops)
    x_taps = taps[pl.ds(0, views), :]
    x_line = jnp.zeros((views, along), F32)
    for j in range(tap_count):
        x_line = jnp.where(index == j, jnp.broadcast_to(x_taps[:, j : j + 1], (views, along)), x_line)
    r_of = lax.broadcasted_iota(I32, (rows, along), 0)
    c_of = lax.broadcasted_iota(I32, (rows, along), 1)
    still = jnp.where(c_of == r_of + rows * hops, 1.0, 0.0)
    for v in range(views):
        line = jnp.broadcast_to(x_line[v : v + 1], (rows, along))
        x = pltpu.roll(line, 0, 1, stride=1, stride_axis=0)
        row = me * rows + r_of - jnp.broadcast_to(shifts[v : v + 1], (rows, along))
        valid = (row >= 0) & (row < slab)
        x_fwd[pl.ds(v * rows, rows), :] = jnp.where(valid, x, still).astype(BF16)
        x_tmp[pl.ds(v * rows, rows), :] = jnp.where(valid, x, 0.0)
    x_tmp[...] = jnp.transpose(x_tmp[...])

    def rows_of(block):
        return x_tmp[pl.ds(pl.multiple_of(block * rows, rows), rows), :].astype(BF16)

    for k in range(3):
        x_adj[pl.ds(k * rows, rows), :] = rows_of(2 * k + 1)
        x_adj[pl.ds((3 + k) * rows, rows), :] = rows_of(2 * k + 2 - 2 * odd)
    x_adj[pl.ds(6 * rows, rows), :] = rows_of(6 * odd)

    width = rows * (2 * hops + 1)

    def forward(j):
        base = pl.multiple_of(j * part, part)
        slabs = []
        for p in range(0, part, 2):
            pair = [win[:, base + p + q].reshape(width, along) for q in range(2)]
            res = dot(x_fwd[:, :width], jnp.concatenate(pair, axis=1)).astype(BF16)
            slabs += [res[:, :along], res[:, along:]]
        for w in range(views // 2):
            both = []
            for v in (2 * w, 2 * w + 1):
                both.append(jnp.concatenate([s[v * rows : (v + 1) * rows] for s in slabs], axis=0))
            res = dot(jnp.concatenate(both, axis=1), z_fwd[w]).astype(BF16)
            for q in range(2):
                block = res[:, q * along : (q + 1) * along].reshape(part, rows, along)
                held[pl.ds((2 * w + q) * rows, rows), pl.ds(base, part), :] = jnp.swapaxes(block, 0, 1)

    @pl.loop(0, PARTS + 2)
    def _(t):
        @pl.when(t < PARTS)
        def _():
            landed(side, t).wait_recv()
            pl.when(beyond)(lambda: onward(t).start())
            pass_near(t).start()

        @pl.when((t >= 1) & (t <= PARTS) & before)
        def _():
            landed(-side, t - 1).wait_recv()
            pass_back(t - 1).start()

        @pl.when(t >= 2)
        def _():
            j = t - 2
            landed(mate, j).wait_recv()
            landed(side + mate, j).wait_recv()
            pl.when(before)(lambda: landed(mate - side, j).wait_recv())
            pl.when(away)(lambda: landed(far, j).wait_recv())
            forward(j)

    load_img.wait()

    @pl.loop(0, views)
    def _(v):
        first = pl.multiple_of(v * rows, rows)
        ratios = []
        blurred = []
        for i in range(0, rows, 2):
            pair = [held[first + i + q] for q in range(2)]
            blurred.append(dot(y_fwd[v], jnp.concatenate(pair, axis=1)))
        for i in range(0, rows, 2):
            image = jnp.concatenate([img[v, i + q].astype(F32) for q in range(2)], axis=1)
            ratios.append((image / blurred[i // 2]).astype(BF16))
        for i in range(0, rows, 2):
            res = dot(y_adj[v], ratios[i // 2]).astype(BF16)
            for q in range(2):
                held[first + i + q] = res[:, q * along : (q + 1) * along]

    def back_send_copy(src, dst, there, kind, j):
        return pltpu.make_async_remote_copy(
            src_ref=src.at[span(j)],
            dst_ref=dst.at[span(j)],
            send_sem=back_send.at[kind, j],
            recv_sem=back_recv.at[kind, j],
            device_id={"blocks": there},
            device_id_type=MESH,
        )

    def to_mate(j):
        return back_send_copy(mate_out, mate_in, me + mate, 0, j)

    def to_far(j):
        return back_send_copy(far_out, far_in, me + far, 1, j)

    def to_on(j):
        return back_send_copy(on_out, on_in, me - 2 * side, 2, j)

    def to_side(j):
        return back_send_copy(dir_out, dir_in, me + side, 3, j)

    def backward(j):
        base = pl.multiple_of(j * part, part)
        cols = []
        for w in range(views // 2):
            both = [
                held[pl.ds((2 * w + q) * rows, rows), pl.ds(base, part), :].reshape(rows * part, along)
                for q in range(2)
            ]
            res = dot(jnp.concatenate(both, axis=1), z_adj[w]).astype(BF16)
            for q in range(2):
                block = res[:, q * along : (q + 1) * along].reshape(rows, part, along)
                cols.append(jnp.swapaxes(block, 0, 1))
        for p in range(0, part, 2):
            pair = [jnp.concatenate([col[p + q] for col in cols], axis=0) for q in range(2)]
            both = dot(x_adj[...], jnp.concatenate(pair, axis=1))
            for q in range(2):
                y = base + p + q
                res = both[:, q * along : (q + 1) * along] * scale[pl.ds(y, 1), :]
                own[y] = res[: 3 * rows]
                mate_out[y] = coded(res[3 * rows : 6 * rows])
                far_out[y] = coded(res[6 * rows :])

    def merge(j):
        base = pl.multiple_of(j * part, part)
        own[pl.ds(base, part)] += decoded(mate_in[pl.ds(base, part)])
        pick = pl.ds(pl.multiple_of(down * rows, rows), rows)

        @pl.when(before)
        def _():
            on_out[pl.ds(base, part)] = coded(own[pl.ds(base, part), pick, :])

    def gather(j):
        base = pl.multiple_of(j * part, part)
        pick = pl.ds(pl.multiple_of(up * rows, rows), rows)
        total = own[pl.ds(base, part), pick, :] + decoded(on_in[pl.ds(base, part)])
        dir_out[pl.ds(base, part)] = coded(total)

    def finish(j):
        base = pl.multiple_of(j * part, part)
        there = pl.ds(base, part)
        total = own[there, pl.ds(rows, rows), :] + decoded(dir_in[there]) + decoded(far_in[there])
        total = jnp.swapaxes(total, 0, 1) * unscale[there, :]
        out_ref[:, there, :] = est[:, there, :] * total

    @pl.loop(0, PARTS + 3)
    def _(t):
        @pl.when(t < PARTS)
        def _():
            backward(t)
            to_mate(t).start()
            pl.when(away)(lambda: to_far(t).start())

        @pl.when((t >= 1) & (t <= PARTS))
        def _():
            j = t - 1
            to_mate(j).wait_recv()
            merge(j)
            pl.when(before)(lambda: to_on(j).start())

        @pl.when((t >= 2) & (t <= PARTS + 1))
        def _():
            j = t - 2
            pl.when(beyond)(lambda: to_on(j).wait_recv())
            gather(j)
            to_side(j).start()

        @pl.when(t >= 3)
        def _():
            j = t - 3
            to_side(j).wait_recv()
            pl.when(away)(lambda: to_far(j).wait_recv())
            finish(j)

    @pl.loop(0, PARTS)
    def _(j):
        direct(j).wait_send()
        near(j).wait_send()
        pass_near(j).wait_send()
        to_mate(j).wait_send()
        to_side(j).wait_send()

        @pl.when(away)
        def _():
            long(j).wait_send()
            to_far(j).wait_send()

        pl.when(beyond)(lambda: onward(j).wait_send())

        @pl.when(before)
        def _():
            pass_back(j).wait_send()
            to_on(j).wait_send()


def body(estimate, images, point_spread, shifts):
    views = images.shape[0]
    rows, across, along = estimate.shape
    tap_count = point_spread.shape[2]
    count = lax.axis_size("blocks")
    hops = -(-(tap_count // 2 + SHIFT) // rows)
    dims = (count, views, rows, across, along, tap_count, hops)
    some = pl.BlockSpec(memory_space=pl.ANY)
    vmem = pl.BlockSpec(memory_space=pltpu.VMEM)
    line = (across, rows, along)
    return pl.pallas_call(
        functools.partial(fused_kernel, dims),
        out_shape=jax.ShapeDtypeStruct(estimate.shape, F32),
        in_specs=[some, some, vmem, pl.BlockSpec(memory_space=pltpu.SMEM)],
        out_specs=vmem,
        scratch_shapes=[
            pltpu.VMEM(estimate.shape, F32),
            pltpu.VMEM(images.shape, BF16),
            pltpu.VMEM((2 * hops + 1,) + line, BF16),
            pltpu.VMEM((views * rows, across, along), BF16),
            pltpu.VMEM((across, 3 * rows, along), F32),
            pltpu.VMEM((across, 3 * rows, along), I16),
            pltpu.VMEM((across, 3 * rows, along), I16),
        ]
        + [pltpu.VMEM(line, I16)] * 6
        + [
            pltpu.VMEM((4 * views, along), F32),
            pltpu.VMEM((views * rows, along), F32),
            pltpu.VMEM((views * rows, along), BF16),
            pltpu.VMEM(((2 * hops + 1) * rows, views * rows), BF16),
            pltpu.VMEM((views // 2, 2 * along, 2 * along), BF16),
            pltpu.VMEM((views // 2, 2 * along, 2 * along), BF16),
            pltpu.VMEM((views, across, across), BF16),
            pltpu.VMEM((views, across, across), BF16),
            pltpu.VMEM((across, along), F32),
            pltpu.VMEM((across, along), F32),
            pltpu.SemaphoreType.DMA((PARTS + 1,)),
            pltpu.SemaphoreType.DMA((6, PARTS)),
            pltpu.SemaphoreType.DMA((2 * hops + 1, PARTS)),
            pltpu.SemaphoreType.DMA((4, PARTS)),
            pltpu.SemaphoreType.DMA((4, PARTS)),
        ],
        compiler_params=pltpu.CompilerParams(
            collective_id=0, has_side_effects=True, vmem_limit_bytes=56 * 1024 * 1024
        ),
        name="restore",
    )(estimate, images, point_spread, shifts)


def solution(mesh):
    in_specs = (
        P(("groups", "blocks"), None, None),
        P(None, ("groups", "blocks"), None, None),
        P(),
        P(),
    )
    out_specs = P(("groups", "blocks"), None, None)
    return jax.shard_map(body, mesh=mesh, in_specs=in_specs, out_specs=out_specs, check_vma=False)
```

```python
import functools

import jax
import jax.numpy as jnp
from jax import lax
from jax.experimental import pallas as pl
from jax.experimental.pallas import tpu as pltpu
from jax.sharding import PartitionSpec as P

SHIFT = 32
PARTS = 8
ARRIVED = (64, 96, 128)
UNROLL = 2
TOP = 4.2
F32 = jnp.float32
BF16 = jnp.bfloat16
I16 = jnp.int16
I32 = jnp.int32
MESH = pl.DeviceIdType.MESH


def dot(a, b):
    return jnp.dot(a, b, preferred_element_type=F32)


def coded(x):
    return ((x + 0.5).astype(I32) - 32768).astype(I16)


def decoded(q):
    return (q.astype(I32) + 32768).astype(F32)


def fused_kernel(
    dims,
    est_hbm,
    img_hbm,
    spread_ref,
    shift_ref,
    out_ref,
    est,
    img,
    win,
    held,
    ratio,
    back,
    own,
    mate_out,
    mate_in,
    far_out,
    far_in,
    on_out,
    on_in,
    dir_out,
    dir_in,
    taps,
    x_tmp,
    x_fwd,
    x_adj,
    z_fwd,
    z_adj,
    y_fwd,
    y_adj,
    scale,
    unscale,
    local_sem,
    send_sem,
    recv_sem,
    back_send,
    back_recv,
):
    count, views, rows, across, along, tap_count, hops = dims
    margin = tap_count // 2
    part = across // PARTS
    mid = hops
    slab = rows * count
    me = lax.axis_index("blocks")
    odd = lax.rem(me, 2)
    right = lax.rem(me, 4) // 2
    mate = 1 - 2 * odd
    far = -3 * mate
    side = 2 - 4 * right
    up = 2 - 2 * right
    down = 2 * right
    beyond = (me + 2 * side >= 0) & (me + 2 * side < count)
    before = (me - 2 * side >= 0) & (me - 2 * side < count)
    away = (me + far >= 0) & (me + far < count)

    barrier = pltpu.get_barrier_semaphore()

    def signal(there):
        pl.semaphore_signal(barrier, inc=1, device_id={"blocks": there}, device_id_type=MESH)

    signal(me + mate)
    signal(me + side)
    pl.when(beyond)(lambda: signal(me + 2 * side))
    pl.when(before)(lambda: signal(me - 2 * side))
    pl.when(away)(lambda: signal(me + far))

    def span(j):
        return pl.ds(pl.multiple_of(j * part, part), part)

    def load_est(j):
        return pltpu.make_async_copy(est_hbm.at[:, span(j)], est.at[:, span(j)], local_sem.at[j])

    load_img = pltpu.make_async_copy(img_hbm, img, local_sem.at[PARTS])

    @pl.loop(0, PARTS)
    def _(j):
        load_est(j).start()

    load_img.start()

    def send(from_slot, to_slot, there, kind, j):
        return pltpu.make_async_remote_copy(
            src_ref=win.at[from_slot, span(j)],
            dst_ref=win.at[to_slot, span(j)],
            send_sem=send_sem.at[kind, j],
            recv_sem=recv_sem.at[to_slot, j],
            device_id={"blocks": there},
            device_id_type=MESH,
        )

    def direct(j):
        return send(mid, mid - side, me + side, 0, j)

    def onward(j):
        return send(mid + side, mid - side, me + 2 * side, 1, j)

    def long(j):
        return send(mid, mid - far, me + far, 2, j)

    def near(j):
        return send(mid, mid - mate, me + mate, 3, j)

    def pass_near(j):
        return send(mid + side, mid + side - mate, me + mate, 4, j)

    def pass_back(j):
        return send(mid - side, mid - side - mate, me + mate, 5, j)

    def landed(offset, j):
        return send(mid, mid + offset, me + mate, 0, j)

    def prepare(j):
        load_est(j).wait()
        win[mid, span(j)] = jnp.swapaxes(est[:, span(j), :].astype(BF16), 0, 1)

    prepare(0)
    peers = 2 + beyond.astype(I32) + before.astype(I32) + away.astype(I32)
    pl.semaphore_wait(barrier, peers)

    @pl.loop(0, PARTS)
    def _(j):
        pl.when(j > 0)(lambda: prepare(j))
        direct(j).start()
        pl.when(away)(lambda: long(j).start())
        near(j).start()

    def build_across():
        for offset in range(-hops, hops + 1):
            there = me + offset
            if offset:

                @pl.when((there < 0) | (there >= count))
                def _():
                    win[mid + offset] = jnp.zeros(win.shape[1:], BF16)

        def none_in(ref):
            ref[...] = jnp.full(ref.shape, -32768, I16)

        pl.when(jnp.logical_not(beyond))(lambda: none_in(on_in))
        pl.when(jnp.logical_not(away))(lambda: none_in(far_in))

        taps[...] = jnp.zeros(taps.shape, F32)
        for v in range(views):
            for a in range(3):
                line = spread_ref[a, pl.ds(v, 1), :]
                total = jnp.sum(line, axis=1, keepdims=True)
                taps[pl.ds(a * views + v, 1), pl.ds(0, tap_count)] = (line / total).astype(BF16).astype(F32)
        every = taps[...].astype(BF16)
        r = lax.broadcasted_iota(I32, (along, along), 0)
        c = lax.broadcasted_iota(I32, (along, along), 1)
        place = jnp.where(c < along // 2, c, c - along)
        plus = dot(every, (r == margin + place).astype(F32).astype(BF16))
        minus = dot(every, (r == margin - place).astype(F32).astype(BF16))
        close = jnp.abs(r - c) <= margin

        def turned(lines, row):
            line = jnp.broadcast_to(lines[row : row + 1], (along, along))
            return jnp.where(close, pltpu.roll(line, 0, 1, stride=1, stride_axis=0), 0.0)

        z_fwd[...] = jnp.zeros(z_fwd.shape, BF16)
        z_adj[...] = jnp.zeros(z_adj.shape, BF16)
        gains = [[], [], []]
        for v in range(views):
            half = pl.ds((v % 2) * along, along)
            for a in range(3):
                m = turned(minus, a * views + v)
                p = turned(plus, a * views + v).astype(BF16)
                inv = 1.0 / jnp.sum(m, axis=0, keepdims=True)
                gains[a].append(dot(jnp.broadcast_to(inv, (16, along)).astype(BF16), p)[:1])
                if a == 1:
                    y_fwd[v] = p
                    y_adj[v] = m.astype(BF16)
                if a == 2:
                    z_fwd[v // 2, half, half] = m.astype(BF16)
                    z_adj[v // 2, half, half] = p
        gain_x, gain_y, gain_z = [jnp.concatenate(g, axis=0) for g in gains]
        left = gain_y * jnp.max(gain_x, axis=1, keepdims=True)
        bound = lax.dot_general(left, gain_z, (((0,), (0,)), ((), ())), preferred_element_type=F32)
        bound = bound * (TOP * 1.03)
        scale[...] = 65535.0 / bound
        unscale[...] = bound / (65535.0 * views)

    def build_rows():
        shifts = jnp.zeros((views, along), I32)
        v_of = lax.broadcasted_iota(I32, (views, along), 0)
        w_of = lax.broadcasted_iota(I32, (views, along), 1)
        for v in range(views):
            shifts = jnp.where(v_of == v, shift_ref[v], shifts)
        index = w_of + shifts + (margin - rows * hops)
        x_taps = taps[pl.ds(0, views), :]
        x_line = jnp.zeros((views, along), F32)
        for j in range(tap_count):
            x_line = jnp.where(index == j, jnp.broadcast_to(x_taps[:, j : j + 1], (views, along)), x_line)
        r_of = lax.broadcasted_iota(I32, (rows, along), 0)
        c_of = lax.broadcasted_iota(I32, (rows, along), 1)
        still = jnp.where(c_of == r_of + rows * hops, 1.0, 0.0)
        for v in range(views):
            line = jnp.broadcast_to(x_line[v : v + 1], (rows, along))
            x = pltpu.roll(line, 0, 1, stride=1, stride_axis=0)
            row = me * rows + r_of - jnp.broadcast_to(shifts[v : v + 1], (rows, along))
            valid = (row >= 0) & (row < slab)
            x_fwd[pl.ds(v * rows, rows), :] = jnp.where(valid, x, still).astype(BF16)
            x_tmp[pl.ds(v * rows, rows), :] = jnp.where(valid, x, 0.0)
        x_tmp[...] = jnp.transpose(x_tmp[...])

        def rows_of(block):
            return x_tmp[pl.ds(pl.multiple_of(block * rows, rows), rows), :].astype(BF16)

        for k in range(3):
            x_adj[pl.ds(k * rows, rows), :] = rows_of(2 * k + 1)
            x_adj[pl.ds((3 + k) * rows, rows), :] = rows_of(2 * k + 2 - 2 * odd)
        x_adj[pl.ds(6 * rows, rows), :] = rows_of(6 * odd)

    width = rows * (2 * hops + 1)

    def forward(j):
        base = pl.multiple_of(j * part, part)
        slabs = []
        for p in range(0, part, 2):
            pair = [win[:, base + p + q].reshape(width, along) for q in range(2)]
            res = dot(x_fwd[:, :width], jnp.concatenate(pair, axis=1)).astype(BF16)
            slabs += [res[:, :along], res[:, along:]]
        for w in range(views // 2):
            both = []
            for v in (2 * w, 2 * w + 1):
                both.append(jnp.concatenate([s[v * rows : (v + 1) * rows] for s in slabs], axis=0))
            res = dot(jnp.concatenate(both, axis=1), z_fwd[w]).astype(BF16)
            for q in range(2):
                block = res[:, q * along : (q + 1) * along].reshape(part, rows, along)
                held[pl.ds((2 * w + q) * rows, rows), pl.ds(base, part), :] = jnp.swapaxes(block, 0, 1)

    def middle(step):
        f0, f1, a0, a1 = step
        w0, w1 = max(0, f0 - part), min(across, f1 + part)
        u0 = max(0, a0 - part)

        @pl.loop(0, views, unroll=UNROLL)
        def _(v):
            first = pl.multiple_of(v * rows, rows)
            blurred = []
            for i in range(0, rows, 2):
                pair = [held[first + i + q, w0:w1] for q in range(2)]
                matrix = y_fwd[v, f0 - w0 : f1 - w0, : w1 - w0]
                blurred.append(dot(matrix, jnp.concatenate(pair, axis=1)))
            ratios = []
            for i in range(0, rows, 2):
                image = jnp.concatenate([img[v, i + q, f0:f1].astype(F32) for q in range(2)], axis=1)
                result = (image / blurred[i // 2]).astype(BF16)
                for q in range(2):
                    ratio[first + i + q, f0:f1] = result[:, q * along : (q + 1) * along]
                if u0 < f0:
                    pair = [ratio[first + i + q, u0:f0] for q in range(2)]
                    result = jnp.concatenate([jnp.concatenate(pair, axis=1), result], axis=0)
                ratios.append(result)
            for i in range(0, rows, 2):
                matrix = y_adj[v, a0 - u0 : a1 - u0, : f1 - u0]
                res = dot(matrix, ratios[i // 2]).astype(BF16)
                for q in range(2):
                    back[first + i + q, a0:a1] = res[:, q * along : (q + 1) * along]

    def back_send_copy(src, dst, there, kind, j):
        return pltpu.make_async_remote_copy(
            src_ref=src.at[span(j)],
            dst_ref=dst.at[span(j)],
            send_sem=back_send.at[kind, j],
            recv_sem=back_recv.at[kind, j],
            device_id={"blocks": there},
            device_id_type=MESH,
        )

    def to_mate(j):
        return back_send_copy(mate_out, mate_in, me + mate, 0, j)

    def to_far(j):
        return back_send_copy(far_out, far_in, me + far, 1, j)

    def to_on(j):
        return back_send_copy(on_out, on_in, me - 2 * side, 2, j)

    def to_side(j):
        return back_send_copy(dir_out, dir_in, me + side, 3, j)

    def backward(j):
        base = pl.multiple_of(j * part, part)
        cols = []
        for w in range(views // 2):
            both = [
                back[pl.ds((2 * w + q) * rows, rows), pl.ds(base, part), :].reshape(rows * part, along)
                for q in range(2)
            ]
            res = dot(jnp.concatenate(both, axis=1), z_adj[w]).astype(BF16)
            for q in range(2):
                block = res[:, q * along : (q + 1) * along].reshape(rows, part, along)
                cols.append(jnp.swapaxes(block, 0, 1))
        for p in range(0, part, 2):
            pair = [jnp.concatenate([col[p + q] for col in cols], axis=0) for q in range(2)]
            both = dot(x_adj[...], jnp.concatenate(pair, axis=1))
            for q in range(2):
                y = base + p + q
                res = both[:, q * along : (q + 1) * along] * scale[pl.ds(y, 1), :]
                own[y] = res[: 3 * rows]
                mate_out[y] = coded(res[3 * rows : 6 * rows])
                far_out[y] = coded(res[6 * rows :])

    def merge(j):
        base = pl.multiple_of(j * part, part)
        own[pl.ds(base, part)] += decoded(mate_in[pl.ds(base, part)])
        pick = pl.ds(pl.multiple_of(down * rows, rows), rows)

        @pl.when(before)
        def _():
            on_out[pl.ds(base, part)] = coded(own[pl.ds(base, part), pick, :])

    def gather(j):
        base = pl.multiple_of(j * part, part)
        pick = pl.ds(pl.multiple_of(up * rows, rows), rows)
        total = own[pl.ds(base, part), pick, :] + decoded(on_in[pl.ds(base, part)])
        dir_out[pl.ds(base, part)] = coded(total)

    def finish(j):
        base = pl.multiple_of(j * part, part)
        there = pl.ds(base, part)
        total = own[there, pl.ds(rows, rows), :] + decoded(dir_in[there]) + decoded(far_in[there])
        out_ref[:, there, :] = jnp.swapaxes(total, 0, 1) * unscale[there, :]

    arrived = [n // part for n in ARRIVED]
    steps = []
    f0, a0 = 0, 0
    for n in ARRIVED:
        f1 = n - part if n < across else across
        a1 = f1 - part if n < across else across
        steps.append((f0, f1, a0, a1))
        f0, a0 = f1, a1
    ready = [0] + [a1 // part for _, _, _, a1 in steps]

    def picked(t, values):
        out = jnp.int32(values[0])
        for n, value in zip(arrived, values[1:]):
            out = jnp.where(t >= n + 1, jnp.int32(value), out)
        return out

    @pl.loop(0, PARTS + 2)
    def _(t):
        @pl.when(t < PARTS)
        def _():
            landed(side, t).wait_recv()
            pl.when(beyond)(lambda: onward(t).start())
            pass_near(t).start()

        @pl.when((t >= 1) & (t <= PARTS) & before)
        def _():
            landed(-side, t - 1).wait_recv()
            pass_back(t - 1).start()

        pl.when(t == 0)(build_across)
        pl.when(t == 1)(build_rows)

        @pl.when(t >= 2)
        def _():
            j = t - 2
            landed(mate, j).wait_recv()
            landed(side + mate, j).wait_recv()
            pl.when(before)(lambda: landed(mate - side, j).wait_recv())
            pl.when(away)(lambda: landed(far, j).wait_recv())
            forward(j)

        for n, step in zip(arrived, steps):

            @pl.when(t == n + 1)
            def _():
                if n == arrived[0]:
                    load_img.wait()
                middle(step)

        low, high = picked(t - 1, ready), picked(t, ready)

        @pl.when(high > low)
        def _():
            @pl.loop(low, high + 1)
            def _(b):
                @pl.when(b < high)
                def _():
                    backward(b)
                    to_mate(b).start()

                @pl.when(b > low)
                def _():
                    j = b - 1
                    to_mate(j).wait_recv()
                    merge(j)
                    pl.when(before)(lambda: to_on(j).start())
                    pl.when(away)(lambda: to_far(j).start())

            @pl.loop(picked(t - 1, [0] + ready[:-1]), low)
            def _(j):
                pl.when(beyond)(lambda: to_on(j).wait_recv())
                gather(j)
                to_side(j).start()

    done = ready[-2]

    @pl.loop(0, PARTS)
    def _(i):
        @pl.when(i < PARTS - done)
        def _():
            j = i + done
            pl.when(beyond)(lambda: to_on(j).wait_recv())
            gather(j)
            to_side(j).start()

        to_side(i).wait_recv()
        pl.when(away)(lambda: to_far(i).wait_recv())
        finish(i)

    @pl.loop(0, PARTS)
    def _(j):
        direct(j).wait_send()
        near(j).wait_send()
        pass_near(j).wait_send()
        to_mate(j).wait_send()
        to_side(j).wait_send()

        @pl.when(away)
        def _():
            long(j).wait_send()
            to_far(j).wait_send()

        pl.when(beyond)(lambda: onward(j).wait_send())

        @pl.when(before)
        def _():
            pass_back(j).wait_send()
            to_on(j).wait_send()


def body(estimate, images, point_spread, shifts):
    views = images.shape[0]
    rows, across, along = estimate.shape
    tap_count = point_spread.shape[2]
    count = lax.axis_size("blocks")
    hops = -(-(tap_count // 2 + SHIFT) // rows)
    dims = (count, views, rows, across, along, tap_count, hops)
    some = pl.BlockSpec(memory_space=pl.ANY)
    vmem = pl.BlockSpec(memory_space=pltpu.VMEM)
    line = (across, rows, along)
    summed = pl.pallas_call(
        functools.partial(fused_kernel, dims),
        out_shape=jax.ShapeDtypeStruct(estimate.shape, F32),
        in_specs=[some, some, vmem, pl.BlockSpec(memory_space=pltpu.SMEM)],
        out_specs=vmem,
        scratch_shapes=[
            pltpu.VMEM(estimate.shape, F32),
            pltpu.VMEM(images.shape, BF16),
            pltpu.VMEM((2 * hops + 1,) + line, BF16),
            pltpu.VMEM((views * rows, across, along), BF16),
            pltpu.VMEM((views * rows, across, along), BF16),
            pltpu.VMEM((views * rows, across, along), BF16),
            pltpu.VMEM((across, 3 * rows, along), F32),
            pltpu.VMEM((across, 3 * rows, along), I16),
            pltpu.VMEM((across, 3 * rows, along), I16),
        ]
        + [pltpu.VMEM(line, I16)] * 6
        + [
            pltpu.VMEM((4 * views, along), F32),
            pltpu.VMEM((views * rows, along), F32),
            pltpu.VMEM((views * rows, along), BF16),
            pltpu.VMEM(((2 * hops + 1) * rows, views * rows), BF16),
            pltpu.VMEM((views // 2, 2 * along, 2 * along), BF16),
            pltpu.VMEM((views // 2, 2 * along, 2 * along), BF16),
            pltpu.VMEM((views, across, across), BF16),
            pltpu.VMEM((views, across, across), BF16),
            pltpu.VMEM((across, along), F32),
            pltpu.VMEM((across, along), F32),
            pltpu.SemaphoreType.DMA((PARTS + 1,)),
            pltpu.SemaphoreType.DMA((6, PARTS)),
            pltpu.SemaphoreType.DMA((2 * hops + 1, PARTS)),
            pltpu.SemaphoreType.DMA((4, PARTS)),
            pltpu.SemaphoreType.DMA((4, PARTS)),
        ],
        compiler_params=pltpu.CompilerParams(
            collective_id=0, has_side_effects=True, vmem_limit_bytes=56 * 1024 * 1024
        ),
        name="restore",
    )(estimate, images, jnp.swapaxes(point_spread, 0, 1), shifts)
    return estimate * summed


def solution(mesh):
    in_specs = (
        P(("groups", "blocks"), None, None),
        P(None, ("groups", "blocks"), None, None),
        P(),
        P(),
    )
    out_specs = P(("groups", "blocks"), None, None)
    return jax.shard_map(body, mesh=mesh, in_specs=in_specs, out_specs=out_specs, check_vma=False)
```

```python
import functools

import jax
import jax.numpy as jnp
from jax import lax
from jax.experimental import pallas as pl
from jax.experimental.pallas import tpu as pltpu
from jax.sharding import PartitionSpec as P

SHIFT = 32
PARTS = 8
AHEAD = 9
MERGE, GATHER, FAR, FINISH = 4, 6, 4, 8
TOP = 4.2
F32 = jnp.float32
BF16 = jnp.bfloat16
I16 = jnp.int16
I32 = jnp.int32
MESH = pl.DeviceIdType.MESH


def dot(a, b):
    return jnp.dot(a, b, preferred_element_type=F32)


def coded(x):
    return ((x + 0.5).astype(I32) - 32768).astype(I16)


def decoded(q):
    return (q.astype(I32) + 32768).astype(F32)


def fused_kernel(
    dims,
    est_hbm,
    img_hbm,
    spread_ref,
    shift_ref,
    out_ref,
    est,
    img,
    win,
    held,
    ratio,
    back,
    own,
    mate_out,
    mate_in,
    far_out,
    far_in,
    on_out,
    on_in,
    dir_out,
    dir_in,
    taps,
    x_tmp,
    x_fwd,
    x_adj,
    z_fwd,
    z_adj,
    y_fwd,
    y_adj,
    scale,
    unscale,
    local_sem,
    send_sem,
    recv_sem,
    back_send,
    back_recv,
):
    count, views, rows, across, along, tap_count, hops = dims
    margin = tap_count // 2
    part = across // PARTS
    mid = hops
    slab = rows * count
    me = lax.axis_index("blocks")
    odd = lax.rem(me, 2)
    right = lax.rem(me, 4) // 2
    mate = 1 - 2 * odd
    far = -3 * mate
    side = 2 - 4 * right
    up = 2 - 2 * right
    down = 2 * right
    beyond = (me + 2 * side >= 0) & (me + 2 * side < count)
    before = (me - 2 * side >= 0) & (me - 2 * side < count)
    away = (me + far >= 0) & (me + far < count)

    barrier = pltpu.get_barrier_semaphore()

    def signal(there):
        pl.semaphore_signal(barrier, inc=1, device_id={"blocks": there}, device_id_type=MESH)

    signal(me + mate)
    signal(me + side)
    pl.when(beyond)(lambda: signal(me + 2 * side))
    pl.when(before)(lambda: signal(me - 2 * side))
    pl.when(away)(lambda: signal(me + far))

    def span(j):
        return pl.ds(pl.multiple_of(j * part, part), part)

    def load_est(j):
        return pltpu.make_async_copy(est_hbm.at[:, span(j)], est.at[:, span(j)], local_sem.at[j])

    load_img = pltpu.make_async_copy(img_hbm, img, local_sem.at[PARTS])

    @pl.loop(0, PARTS)
    def _(j):
        load_est(j).start()

    load_img.start()

    def send(from_slot, to_slot, there, kind, j):
        return pltpu.make_async_remote_copy(
            src_ref=win.at[from_slot, span(j)],
            dst_ref=win.at[to_slot, span(j)],
            send_sem=send_sem.at[kind, j],
            recv_sem=recv_sem.at[to_slot, j],
            device_id={"blocks": there},
            device_id_type=MESH,
        )

    def direct(j):
        return send(mid, mid - side, me + side, 0, j)

    def onward(j):
        return send(mid + side, mid - side, me + 2 * side, 1, j)

    def long(j):
        return send(mid, mid - far, me + far, 2, j)

    def near(j):
        return send(mid, mid - mate, me + mate, 3, j)

    def pass_near(j):
        return send(mid + side, mid + side - mate, me + mate, 4, j)

    def pass_back(j):
        return send(mid - side, mid - side - mate, me + mate, 5, j)

    def landed(offset, j):
        return send(mid, mid + offset, me + mate, 0, j)

    def prepare(j):
        load_est(j).wait()
        win[mid, span(j)] = jnp.swapaxes(est[:, span(j), :].astype(BF16), 0, 1)

    prepare(0)
    peers = 2 + beyond.astype(I32) + before.astype(I32) + away.astype(I32)
    pl.semaphore_wait(barrier, peers)

    @pl.loop(0, PARTS)
    def _(j):
        pl.when(j > 0)(lambda: prepare(j))
        direct(j).start()
        pl.when(away)(lambda: long(j).start())
        near(j).start()

    def build_across():
        for offset in range(-hops, hops + 1):
            there = me + offset
            if offset:

                @pl.when((there < 0) | (there >= count))
                def _():
                    win[mid + offset] = jnp.zeros(win.shape[1:], BF16)

        def none_in(ref):
            ref[...] = jnp.full(ref.shape, -32768, I16)

        for edge in (0, across + part):
            held[:, edge : edge + part] = jnp.zeros((views * rows, part, along), BF16)
            ratio[:, edge : edge + part] = jnp.zeros((views * rows, part, along), BF16)

        pl.when(jnp.logical_not(beyond))(lambda: none_in(on_in))
        pl.when(jnp.logical_not(away))(lambda: none_in(far_in))

        every = taps[...].astype(BF16)
        r = lax.broadcasted_iota(I32, (along, along), 0)
        c = lax.broadcasted_iota(I32, (along, along), 1)
        place = jnp.where(c < along // 2, c, c - along)
        plus = dot(every, (r == margin + place).astype(F32).astype(BF16))
        minus = dot(every, (r == margin - place).astype(F32).astype(BF16))
        close = jnp.abs(r - c) <= margin

        def turned(lines, row):
            line = jnp.broadcast_to(lines[row : row + 1], (along, along))
            return jnp.where(close, pltpu.roll(line, 0, 1, stride=1, stride_axis=0), 0.0)

        z_fwd[...] = jnp.zeros(z_fwd.shape, BF16)
        z_adj[...] = jnp.zeros(z_adj.shape, BF16)
        gains = [[], [], []]
        for v in range(views):
            half = pl.ds((v % 2) * along, along)
            for a in range(3):
                m = turned(minus, a * views + v)
                p = turned(plus, a * views + v).astype(BF16)
                inv = 1.0 / jnp.sum(m, axis=0, keepdims=True)
                gains[a].append(dot(jnp.broadcast_to(inv, (16, along)).astype(BF16), p)[:1])
                if a == 1:
                    y_fwd[v] = p[part : 2 * part]
                    y_adj[v] = m[part : 2 * part].astype(BF16)
                if a == 2:
                    z_fwd[v // 2, half, half] = m.astype(BF16)
                    z_adj[v // 2, half, half] = p
        gain_x, gain_y, gain_z = [jnp.concatenate(g, axis=0) for g in gains]
        left = gain_y * jnp.max(gain_x, axis=1, keepdims=True)
        bound = lax.dot_general(left, gain_z, (((0,), (0,)), ((), ())), preferred_element_type=F32)
        bound = bound * (TOP * 1.03)
        scale[...] = 65535.0 / bound
        unscale[...] = bound / (65535.0 * views)

    def build_rows():
        taps[...] = jnp.zeros(taps.shape, F32)
        for v in range(views):
            for a in range(3):
                line = spread_ref[a, pl.ds(v, 1), :]
                total = jnp.sum(line, axis=1, keepdims=True)
                taps[pl.ds(a * views + v, 1), pl.ds(0, tap_count)] = (line / total).astype(BF16).astype(F32)

        shifts = jnp.zeros((views, along), I32)
        v_of = lax.broadcasted_iota(I32, (views, along), 0)
        w_of = lax.broadcasted_iota(I32, (views, along), 1)
        for v in range(views):
            shifts = jnp.where(v_of == v, shift_ref[v], shifts)
        index = w_of + shifts + (margin - rows * hops)
        x_taps = taps[pl.ds(0, views), :]
        x_line = jnp.zeros((views, along), F32)
        for j in range(tap_count):
            x_line = jnp.where(index == j, jnp.broadcast_to(x_taps[:, j : j + 1], (views, along)), x_line)
        r_of = lax.broadcasted_iota(I32, (rows, along), 0)
        c_of = lax.broadcasted_iota(I32, (rows, along), 1)
        still = jnp.where(c_of == r_of + rows * hops, 1.0, 0.0)
        for v in range(views):
            line = jnp.broadcast_to(x_line[v : v + 1], (rows, along))
            x = pltpu.roll(line, 0, 1, stride=1, stride_axis=0)
            row = me * rows + r_of - jnp.broadcast_to(shifts[v : v + 1], (rows, along))
            valid = (row >= 0) & (row < slab)
            x_fwd[pl.ds(v * rows, rows), :] = jnp.where(valid, x, still).astype(BF16)
            x_tmp[pl.ds(v * rows, rows), :] = jnp.where(valid, x, 0.0)
        x_tmp[...] = jnp.transpose(x_tmp[...])

        def rows_of(block):
            return x_tmp[pl.ds(pl.multiple_of(block * rows, rows), rows), :].astype(BF16)

        for k in range(3):
            x_adj[pl.ds(k * rows, rows), :] = rows_of(2 * k + 1)
            x_adj[pl.ds((3 + k) * rows, rows), :] = rows_of(2 * k + 2 - 2 * odd)
        x_adj[pl.ds(6 * rows, rows), :] = rows_of(6 * odd)

    width = rows * (2 * hops + 1)

    def forward(j):
        base = pl.multiple_of(j * part, part)
        slabs = []
        for p in range(0, part, 2):
            pair = [win[:, base + p + q].reshape(width, along) for q in range(2)]
            res = dot(x_fwd[:, :width], jnp.concatenate(pair, axis=1)).astype(BF16)
            slabs += [res[:, :along], res[:, along:]]
        for w in range(views // 2):
            both = []
            for v in (2 * w, 2 * w + 1):
                both.append(jnp.concatenate([s[v * rows : (v + 1) * rows] for s in slabs], axis=0))
            res = dot(jnp.concatenate(both, axis=1), z_fwd[w]).astype(BF16)
            for q in range(2):
                block = res[:, q * along : (q + 1) * along].reshape(part, rows, along)
                there = pl.ds(pl.multiple_of(base + part, part), part)
                held[pl.ds((2 * w + q) * rows, rows), there, :] = jnp.swapaxes(block, 0, 1)

    def divide(j):
        out = pl.ds(pl.multiple_of((j + 1) * part, part), part)
        window = pl.ds(pl.multiple_of(j * part, part), 3 * part)
        for v in range(views):
            for i in range(0, rows, 2):
                pair = [held[v * rows + i + q, window] for q in range(2)]
                blurred = dot(y_fwd[v, :, : 3 * part], jnp.concatenate(pair, axis=1))
                image = jnp.concatenate([img[v, i + q, span(j)].astype(F32) for q in range(2)], axis=1)
                result = (image / blurred).astype(BF16)
                for q in range(2):
                    ratio[v * rows + i + q, out] = result[:, q * along : (q + 1) * along]

    def spread_back(j):
        window = pl.ds(pl.multiple_of(j * part, part), 3 * part)
        for v in range(views):
            for i in range(0, rows, 2):
                pair = [ratio[v * rows + i + q, window] for q in range(2)]
                res = dot(y_adj[v, :, : 3 * part], jnp.concatenate(pair, axis=1)).astype(BF16)
                for q in range(2):
                    back[v * rows + i + q] = res[:, q * along : (q + 1) * along]

    def back_send_copy(src, dst, there, kind, j):
        return pltpu.make_async_remote_copy(
            src_ref=src.at[span(j)],
            dst_ref=dst.at[span(j)],
            send_sem=back_send.at[kind, j],
            recv_sem=back_recv.at[kind, j],
            device_id={"blocks": there},
            device_id_type=MESH,
        )

    def to_mate(j):
        return back_send_copy(mate_out, mate_in, me + mate, 0, j)

    def to_far(j):
        return back_send_copy(far_out, far_in, me + far, 1, j)

    def to_on(j):
        return back_send_copy(on_out, on_in, me - 2 * side, 2, j)

    def to_side(j):
        return back_send_copy(dir_out, dir_in, me + side, 3, j)

    def backward(j):
        base = pl.multiple_of(j * part, part)
        cols = []
        for w in range(views // 2):
            both = [
                back[pl.ds((2 * w + q) * rows, rows)].reshape(rows * part, along)
                for q in range(2)
            ]
            res = dot(jnp.concatenate(both, axis=1), z_adj[w]).astype(BF16)
            for q in range(2):
                block = res[:, q * along : (q + 1) * along].reshape(rows, part, along)
                cols.append(jnp.swapaxes(block, 0, 1))
        for p in range(0, part, 2):
            pair = [jnp.concatenate([col[p + q] for col in cols], axis=0) for q in range(2)]
            both = dot(x_adj[...], jnp.concatenate(pair, axis=1))
            for q in range(2):
                y = base + p + q
                res = both[:, q * along : (q + 1) * along] * scale[pl.ds(y, 1), :]
                own[y] = res[: 3 * rows]
                mate_out[y] = coded(res[3 * rows : 6 * rows])
                far_out[y] = coded(res[6 * rows :])

    def merge(j):
        base = pl.multiple_of(j * part, part)
        own[pl.ds(base, part)] += decoded(mate_in[pl.ds(base, part)])
        pick = pl.ds(pl.multiple_of(down * rows, rows), rows)

        @pl.when(before)
        def _():
            on_out[pl.ds(base, part)] = coded(own[pl.ds(base, part), pick, :])

    def gather(j):
        base = pl.multiple_of(j * part, part)
        pick = pl.ds(pl.multiple_of(up * rows, rows), rows)
        total = own[pl.ds(base, part), pick, :] + decoded(on_in[pl.ds(base, part)])
        dir_out[pl.ds(base, part)] = coded(total)

    def finish(j):
        base = pl.multiple_of(j * part, part)
        there = pl.ds(base, part)
        total = own[there, pl.ds(rows, rows), :] + decoded(dir_in[there]) + decoded(far_in[there])
        out_ref[:, there, :] = jnp.swapaxes(total, 0, 1) * unscale[there, :]

    def relay(j):
        landed(side, j).wait_recv()
        pl.when(beyond)(lambda: onward(j).start())
        pass_near(j).start()

    def ahead(t):
        return jnp.minimum(PARTS, (3 * t + AHEAD) // 2)

    build_rows()
    relay(0)
    build_across()

    @pl.loop(0, PARTS + FINISH)
    def _(t):
        def step(lag):
            j = t - lag
            return pl.when((j >= 0) & (j < PARTS)), j

        first = jnp.where(t == 0, 1, ahead(t - 1))
        pl.loop(first, jnp.maximum(first, ahead(t)))(relay)

        now, _ = step(0)

        @now
        def _():
            @pl.when(before)
            def _():
                landed(-side, t).wait_recv()
                pass_back(t).start()

        now, a = step(1)

        @now
        def _():
            landed(mate, a).wait_recv()
            landed(side + mate, a).wait_recv()
            pl.when(before)(lambda: landed(mate - side, a).wait_recv())
            pl.when(away)(lambda: landed(far, a).wait_recv())
            forward(a)

        pl.when(t == 2)(load_img.wait)
        now, b = step(2)
        now(lambda: divide(b))
        now, c = step(3)

        @now
        def _():
            spread_back(c)
            backward(c)
            to_mate(c).start()

        now, d = step(MERGE)

        @now
        def _():
            to_mate(d).wait_recv()
            merge(d)
            pl.when(before)(lambda: to_on(d).start())

        now, e = step(FAR)
        now(lambda: pl.when(away)(lambda: to_far(e).start()))
        now, f = step(GATHER)

        @now
        def _():
            pl.when(beyond)(lambda: to_on(f).wait_recv())
            gather(f)
            to_side(f).start()

        now, g = step(FINISH)

        @now
        def _():
            to_side(g).wait_recv()
            pl.when(away)(lambda: to_far(g).wait_recv())
            finish(g)

    @pl.loop(0, PARTS)
    def _(j):
        direct(j).wait_send()
        near(j).wait_send()
        pass_near(j).wait_send()
        to_mate(j).wait_send()
        to_side(j).wait_send()

        @pl.when(away)
        def _():
            long(j).wait_send()
            to_far(j).wait_send()

        pl.when(beyond)(lambda: onward(j).wait_send())

        @pl.when(before)
        def _():
            pass_back(j).wait_send()
            to_on(j).wait_send()


def body(estimate, images, point_spread, shifts):
    views = images.shape[0]
    rows, across, along = estimate.shape
    tap_count = point_spread.shape[2]
    count = lax.axis_size("blocks")
    hops = -(-(tap_count // 2 + SHIFT) // rows)
    dims = (count, views, rows, across, along, tap_count, hops)
    some = pl.BlockSpec(memory_space=pltpu.HBM)
    vmem = pl.BlockSpec(memory_space=pltpu.VMEM)
    line = (across, rows, along)
    part = across // PARTS
    summed = pl.pallas_call(
        functools.partial(fused_kernel, dims),
        out_shape=jax.ShapeDtypeStruct(estimate.shape, F32),
        in_specs=[some, some, vmem, pl.BlockSpec(memory_space=pltpu.SMEM)],
        out_specs=vmem,
        scratch_shapes=[
            pltpu.VMEM(estimate.shape, F32),
            pltpu.VMEM(images.shape, BF16),
            pltpu.VMEM((2 * hops + 1,) + line, BF16),
            pltpu.VMEM((views * rows, across + 2 * part, along), BF16),
            pltpu.VMEM((views * rows, across + 2 * part, along), BF16),
            pltpu.VMEM((views * rows, part, along), BF16),
            pltpu.VMEM((across, 3 * rows, along), F32),
            pltpu.VMEM((across, 3 * rows, along), I16),
            pltpu.VMEM((across, 3 * rows, along), I16),
        ]
        + [pltpu.VMEM(line, I16)] * 6
        + [
            pltpu.VMEM((4 * views, along), F32),
            pltpu.VMEM((views * rows, along), F32),
            pltpu.VMEM((views * rows, along), BF16),
            pltpu.VMEM(((2 * hops + 1) * rows, views * rows), BF16),
            pltpu.VMEM((views // 2, 2 * along, 2 * along), BF16),
            pltpu.VMEM((views // 2, 2 * along, 2 * along), BF16),
            pltpu.VMEM((views, part, across), BF16),
            pltpu.VMEM((views, part, across), BF16),
            pltpu.VMEM((across, along), F32),
            pltpu.VMEM((across, along), F32),
            pltpu.SemaphoreType.DMA((PARTS + 1,)),
            pltpu.SemaphoreType.DMA((6, PARTS)),
            pltpu.SemaphoreType.DMA((2 * hops + 1, PARTS)),
            pltpu.SemaphoreType.DMA((4, PARTS)),
            pltpu.SemaphoreType.DMA((4, PARTS)),
        ],
        compiler_params=pltpu.CompilerParams(
            collective_id=0, has_side_effects=True, vmem_limit_bytes=52 * 1024 * 1024
        ),
        name="restore",
    )(estimate, images, jnp.swapaxes(point_spread, 0, 1), shifts)
    return estimate * summed


def solution(mesh):
    in_specs = (
        P(("groups", "blocks"), None, None),
        P(None, ("groups", "blocks"), None, None),
        P(),
        P(),
    )
    out_specs = P(("groups", "blocks"), None, None)
    return jax.shard_map(body, mesh=mesh, in_specs=in_specs, out_specs=out_specs, check_vma=False)
```

```python
import functools

import jax
import jax.numpy as jnp
from jax import lax
from jax.experimental import pallas as pl
from jax.experimental.pallas import tpu as pltpu
from jax.sharding import PartitionSpec as P

SHIFT = 32
PARTS = 8
AHEAD = 9
MERGE, GATHER, FAR, FINISH = 4, 6, 4, 8
MAIN, HALT, STAY = 3, 9, 7
TOP = 4.2
F32 = jnp.float32
BF16 = jnp.bfloat16
I16 = jnp.int16
I32 = jnp.int32
MESH = pl.DeviceIdType.MESH


def dot(a, b):
    return jnp.dot(a, b, preferred_element_type=F32)


def coded(x):
    return ((x + 0.5).astype(I32) - 32768).astype(I16)


def decoded(q):
    return (q.astype(I32) + 32768).astype(F32)


def fused_kernel(
    dims,
    est_hbm,
    img_hbm,
    spread_hbm,
    shift_hbm,
    out_ref,
    est,
    img,
    win,
    held,
    ratio,
    back,
    own,
    mate_out,
    mate_in,
    far_out,
    far_in,
    on_out,
    on_in,
    dir_out,
    dir_in,
    taps,
    x_tmp,
    x_fwd,
    x_adj,
    z_fwd,
    z_adj,
    y_fwd,
    y_adj,
    scale,
    unscale,
    spread_ref,
    shift_ref,
    local_sem,
    send_sem,
    recv_sem,
    back_send,
    back_recv,
):
    count, views, rows, across, along, tap_count, hops = dims
    margin = tap_count // 2
    part = across // PARTS
    mid = hops
    slab = rows * count
    me = lax.axis_index("blocks")
    odd = lax.rem(me, 2)
    right = lax.rem(me, 4) // 2
    mate = 1 - 2 * odd
    far = -3 * mate
    side = 2 - 4 * right
    up = 2 - 2 * right
    down = 2 * right
    beyond = (me + 2 * side >= 0) & (me + 2 * side < count)
    before = (me - 2 * side >= 0) & (me - 2 * side < count)
    away = (me + far >= 0) & (me + far < count)

    barrier = pltpu.get_barrier_semaphore()

    def signal(there):
        pl.semaphore_signal(barrier, inc=1, device_id={"blocks": there}, device_id_type=MESH)

    signal(me + mate)
    signal(me + side)
    pl.when(beyond)(lambda: signal(me + 2 * side))
    pl.when(before)(lambda: signal(me - 2 * side))
    pl.when(away)(lambda: signal(me + far))

    def span(j):
        return pl.ds(pl.multiple_of(j * part, part), part)

    def load_est(j):
        return pltpu.make_async_copy(est_hbm.at[:, span(j)], est.at[:, span(j)], local_sem.at[j])

    load_img = pltpu.make_async_copy(img_hbm, img, local_sem.at[PARTS])

    @pl.loop(0, PARTS)
    def _(j):
        load_est(j).start()

    load_spread = pltpu.make_async_copy(spread_hbm, spread_ref, local_sem.at[PARTS + 1])
    load_shift = pltpu.make_async_copy(shift_hbm, shift_ref, local_sem.at[PARTS + 2])
    load_spread.start()
    load_shift.start()
    load_img.start()

    def send(from_slot, to_slot, there, kind, j):
        return pltpu.make_async_remote_copy(
            src_ref=win.at[from_slot, span(j)],
            dst_ref=win.at[to_slot, span(j)],
            send_sem=send_sem.at[kind, j],
            recv_sem=recv_sem.at[to_slot, j],
            device_id={"blocks": there},
            device_id_type=MESH,
        )

    def direct(j):
        return send(mid, mid - side, me + side, 0, j)

    def onward(j):
        return send(mid + side, mid - side, me + 2 * side, 1, j)

    def long(j):
        return send(mid, mid - far, me + far, 2, j)

    def near(j):
        return send(mid, mid - mate, me + mate, 3, j)

    def pass_near(j):
        return send(mid + side, mid + side - mate, me + mate, 4, j)

    def pass_back(j):
        return send(mid - side, mid - side - mate, me + mate, 5, j)

    def landed(offset, j):
        return send(mid, mid + offset, me + mate, 0, j)

    def prepare(j):
        load_est(j).wait()
        win[mid, span(j)] = jnp.swapaxes(est[:, span(j), :].astype(BF16), 0, 1)

    prepare(0)
    peers = 2 + beyond.astype(I32) + before.astype(I32) + away.astype(I32)
    pl.semaphore_wait(barrier, peers)

    @pl.loop(0, PARTS)
    def _(j):
        pl.when(j > 0)(lambda: prepare(j))
        direct(j).start()
        pl.when(away)(lambda: long(j).start())
        near(j).start()

    def build_across():
        for offset in range(-hops, hops + 1):
            there = me + offset
            if offset:

                @pl.when((there < 0) | (there >= count))
                def _():
                    win[mid + offset] = jnp.zeros(win.shape[1:], BF16)

        def none_in(ref):
            ref[...] = jnp.full(ref.shape, -32768, I16)

        for edge in (0, across + part):
            held[:, edge : edge + part] = jnp.zeros((views * rows, part, along), BF16)
            ratio[:, edge : edge + part] = jnp.zeros((views * rows, part, along), BF16)

        pl.when(jnp.logical_not(beyond))(lambda: none_in(on_in))
        pl.when(jnp.logical_not(away))(lambda: none_in(far_in))

        every = taps[...].astype(BF16)
        r = lax.broadcasted_iota(I32, (along, along), 0)
        c = lax.broadcasted_iota(I32, (along, along), 1)
        place = jnp.where(c < along // 2, c, c - along)
        plus = dot(every, (r == margin + place).astype(F32).astype(BF16))
        minus = dot(every, (r == margin - place).astype(F32).astype(BF16))
        close = jnp.abs(r - c) <= margin

        def turned(lines, row):
            line = jnp.broadcast_to(lines[row : row + 1], (along, along))
            return jnp.where(close, pltpu.roll(line, 0, 1, stride=1, stride_axis=0), 0.0)

        z_fwd[...] = jnp.zeros(z_fwd.shape, BF16)
        z_adj[...] = jnp.zeros(z_adj.shape, BF16)
        gains = [[], [], []]
        for v in range(views):
            half = pl.ds((v % 2) * along, along)
            for a in range(3):
                m = turned(minus, a * views + v)
                p = turned(plus, a * views + v).astype(BF16)
                inv = 1.0 / jnp.sum(m, axis=0, keepdims=True)
                gains[a].append(dot(jnp.broadcast_to(inv, (16, along)).astype(BF16), p)[:1])
                if a == 1:
                    y_fwd[v] = p[part : 2 * part]
                    y_adj[v] = m[part : 2 * part].astype(BF16)
                if a == 2:
                    z_fwd[v // 2, half, half] = m.astype(BF16)
                    z_adj[v // 2, half, half] = p
        gain_x, gain_y, gain_z = [jnp.concatenate(g, axis=0) for g in gains]
        left = gain_y * jnp.max(gain_x, axis=1, keepdims=True)
        bound = lax.dot_general(left, gain_z, (((0,), (0,)), ((), ())), preferred_element_type=F32)
        bound = bound * (TOP * 1.03)
        scale[...] = 65535.0 / bound
        unscale[...] = bound / (65535.0 * views)

    def build_rows():
        taps[...] = jnp.zeros(taps.shape, F32)
        for v in range(views):
            for a in range(3):
                line = spread_ref[a, pl.ds(v, 1), :]
                total = jnp.sum(line, axis=1, keepdims=True)
                taps[pl.ds(a * views + v, 1), pl.ds(0, tap_count)] = (line / total).astype(BF16).astype(F32)

        shifts = jnp.zeros((views, along), I32)
        v_of = lax.broadcasted_iota(I32, (views, along), 0)
        w_of = lax.broadcasted_iota(I32, (views, along), 1)
        for v in range(views):
            shifts = jnp.where(v_of == v, shift_ref[v], shifts)
        index = w_of + shifts + (margin - rows * hops)
        x_taps = taps[pl.ds(0, views), :]
        x_line = jnp.zeros((views, along), F32)
        for j in range(tap_count):
            x_line = jnp.where(index == j, jnp.broadcast_to(x_taps[:, j : j + 1], (views, along)), x_line)
        r_of = lax.broadcasted_iota(I32, (rows, along), 0)
        c_of = lax.broadcasted_iota(I32, (rows, along), 1)
        still = jnp.where(c_of == r_of + rows * hops, 1.0, 0.0)
        for v in range(views):
            line = jnp.broadcast_to(x_line[v : v + 1], (rows, along))
            x = pltpu.roll(line, 0, 1, stride=1, stride_axis=0)
            row = me * rows + r_of - jnp.broadcast_to(shifts[v : v + 1], (rows, along))
            valid = (row >= 0) & (row < slab)
            x_fwd[pl.ds(v * rows, rows), :] = jnp.where(valid, x, still).astype(BF16)
            x_tmp[pl.ds(v * rows, rows), :] = jnp.where(valid, x, 0.0)
        x_tmp[...] = jnp.transpose(x_tmp[...])

        def rows_of(block):
            return x_tmp[pl.ds(pl.multiple_of(block * rows, rows), rows), :].astype(BF16)

        for k in range(3):
            x_adj[pl.ds(k * rows, rows), :] = rows_of(2 * k + 1)
            x_adj[pl.ds((3 + k) * rows, rows), :] = rows_of(2 * k + 2 - 2 * odd)
        x_adj[pl.ds(6 * rows, rows), :] = rows_of(6 * odd)

    width = rows * (2 * hops + 1)

    def forward(j):
        base = pl.multiple_of(j * part, part)
        slabs = []
        for p in range(0, part, 2):
            pair = [win[:, base + p + q].reshape(width, along) for q in range(2)]
            res = dot(x_fwd[:, :width], jnp.concatenate(pair, axis=1)).astype(BF16)
            slabs += [res[:, :along], res[:, along:]]
        for w in range(views // 2):
            both = []
            for v in (2 * w, 2 * w + 1):
                both.append(jnp.concatenate([s[v * rows : (v + 1) * rows] for s in slabs], axis=0))
            res = dot(jnp.concatenate(both, axis=1), z_fwd[w]).astype(BF16)
            for q in range(2):
                block = res[:, q * along : (q + 1) * along].reshape(part, rows, along)
                there = pl.ds(pl.multiple_of(base + part, part), part)
                held[pl.ds((2 * w + q) * rows, rows), there, :] = jnp.swapaxes(block, 0, 1)

    def divide(j):
        out = pl.ds(pl.multiple_of((j + 1) * part, part), part)
        window = pl.ds(pl.multiple_of(j * part, part), 3 * part)
        for v in range(views):
            for i in range(0, rows, 2):
                pair = [held[v * rows + i + q, window] for q in range(2)]
                blurred = dot(y_fwd[v, :, : 3 * part], jnp.concatenate(pair, axis=1))
                image = jnp.concatenate([img[v, i + q, span(j)].astype(F32) for q in range(2)], axis=1)
                result = (image / blurred).astype(BF16)
                for q in range(2):
                    ratio[v * rows + i + q, out] = result[:, q * along : (q + 1) * along]

    def spread_back(j):
        window = pl.ds(pl.multiple_of(j * part, part), 3 * part)
        for v in range(views):
            for i in range(0, rows, 2):
                pair = [ratio[v * rows + i + q, window] for q in range(2)]
                res = dot(y_adj[v, :, : 3 * part], jnp.concatenate(pair, axis=1)).astype(BF16)
                for q in range(2):
                    back[v * rows + i + q] = res[:, q * along : (q + 1) * along]

    def back_send_copy(src, dst, there, kind, j):
        return pltpu.make_async_remote_copy(
            src_ref=src.at[span(j)],
            dst_ref=dst.at[span(j)],
            send_sem=back_send.at[kind, j],
            recv_sem=back_recv.at[kind, j],
            device_id={"blocks": there},
            device_id_type=MESH,
        )

    def to_mate(j):
        return back_send_copy(mate_out, mate_in, me + mate, 0, j)

    def to_far(j):
        return back_send_copy(far_out, far_in, me + far, 1, j)

    def to_on(j):
        return back_send_copy(on_out, on_in, me - 2 * side, 2, j)

    def to_side(j):
        return back_send_copy(dir_out, dir_in, me + side, 3, j)

    def backward(j):
        base = pl.multiple_of(j * part, part)
        cols = []
        for w in range(views // 2):
            both = [
                back[pl.ds((2 * w + q) * rows, rows)].reshape(rows * part, along)
                for q in range(2)
            ]
            res = dot(jnp.concatenate(both, axis=1), z_adj[w]).astype(BF16)
            for q in range(2):
                block = res[:, q * along : (q + 1) * along].reshape(rows, part, along)
                cols.append(jnp.swapaxes(block, 0, 1))
        for p in range(0, part, 2):
            pair = [jnp.concatenate([col[p + q] for col in cols], axis=0) for q in range(2)]
            both = dot(x_adj[...], jnp.concatenate(pair, axis=1))
            for q in range(2):
                y = base + p + q
                res = both[:, q * along : (q + 1) * along] * scale[pl.ds(y, 1), :]
                own[y] = res[: 3 * rows]
                mate_out[y] = coded(res[3 * rows : 6 * rows])
                far_out[y] = coded(res[6 * rows :])

    def merge(j):
        base = pl.multiple_of(j * part, part)
        own[pl.ds(base, part)] += decoded(mate_in[pl.ds(base, part)])
        pick = pl.ds(pl.multiple_of(down * rows, rows), rows)

        @pl.when(before)
        def _():
            on_out[pl.ds(base, part)] = coded(own[pl.ds(base, part), pick, :])

    def gather(j):
        base = pl.multiple_of(j * part, part)
        pick = pl.ds(pl.multiple_of(up * rows, rows), rows)
        total = own[pl.ds(base, part), pick, :] + decoded(on_in[pl.ds(base, part)])
        dir_out[pl.ds(base, part)] = coded(total)

    def finish(j):
        base = pl.multiple_of(j * part, part)
        there = pl.ds(base, part)
        total = own[there, pl.ds(rows, rows), :] + decoded(dir_in[there]) + decoded(far_in[there])
        out_ref[:, there, :] = jnp.swapaxes(total, 0, 1) * unscale[there, :]

    def combine(j):
        to_mate(j).wait_recv()
        merge(j)
        pl.when(before)(lambda: to_on(j).start())

    def collect(j):
        pl.when(beyond)(lambda: to_on(j).wait_recv())
        gather(j)
        to_side(j).start()

    def close(j):
        to_side(j).wait_recv()
        pl.when(away)(lambda: to_far(j).wait_recv())
        finish(j)

    def relay(j):
        landed(side, j).wait_recv()
        pl.when(beyond)(lambda: onward(j).start())
        pass_near(j).start()

    def ahead(t):
        return jnp.minimum(PARTS, (3 * t + AHEAD) // 2)

    load_spread.wait()
    load_shift.wait()
    build_rows()
    relay(0)
    build_across()

    @pl.loop(0, PARTS + MAIN)
    def _(t):
        def step(lag):
            j = t - lag
            return pl.when((j >= 0) & (j < PARTS)), j

        first = jnp.where(t == 0, 1, ahead(t - 1))
        pl.loop(first, jnp.maximum(first, ahead(t)))(relay)

        now, _ = step(0)

        @now
        def _():
            @pl.when(before)
            def _():
                landed(-side, t).wait_recv()
                pass_back(t).start()

        now, a = step(1)

        @now
        def _():
            landed(mate, a).wait_recv()
            landed(side + mate, a).wait_recv()
            pl.when(before)(lambda: landed(mate - side, a).wait_recv())
            pl.when(away)(lambda: landed(far, a).wait_recv())
            forward(a)

        pl.when(t == 2)(load_img.wait)
        now, b = step(2)
        now(lambda: divide(b))
        now, c = step(3)

        @now
        def _():
            spread_back(c)
            backward(c)
            to_mate(c).start()

        now, d = step(MERGE)

        now(lambda: combine(d))
        now, e = step(FAR)
        now(lambda: pl.when(away)(lambda: to_far(e).start()))
        now, f = step(GATHER)
        pl.when(t <= HALT)(lambda: now(lambda: collect(f)))
        now, g = step(FINISH)
        pl.when(t <= STAY)(lambda: now(lambda: close(g)))

    for d in range(PARTS + MAIN - MERGE, PARTS):
        combine(d)
    for e in range(PARTS + MAIN - FAR, PARTS):
        pl.when(away)(lambda: to_far(e).start())
    late = HALT - GATHER + 1
    done = max(0, STAY - FINISH + 1)

    @pl.loop(0, PARTS - done)
    def _(i):
        pl.when(i + late < PARTS)(lambda: collect(i + late))
        close(i + done)

    @pl.loop(0, PARTS)
    def _(j):
        direct(j).wait_send()
        near(j).wait_send()
        pass_near(j).wait_send()
        to_mate(j).wait_send()
        to_side(j).wait_send()

        @pl.when(away)
        def _():
            long(j).wait_send()
            to_far(j).wait_send()

        pl.when(beyond)(lambda: onward(j).wait_send())

        @pl.when(before)
        def _():
            pass_back(j).wait_send()
            to_on(j).wait_send()


def body(estimate, images, point_spread, shifts):
    views = images.shape[0]
    rows, across, along = estimate.shape
    tap_count = point_spread.shape[2]
    count = lax.axis_size("blocks")
    hops = -(-(tap_count // 2 + SHIFT) // rows)
    dims = (count, views, rows, across, along, tap_count, hops)
    some = pl.BlockSpec(memory_space=pltpu.HBM)
    vmem = pl.BlockSpec(memory_space=pltpu.VMEM)
    line = (across, rows, along)
    part = across // PARTS
    summed = pl.pallas_call(
        functools.partial(fused_kernel, dims),
        out_shape=jax.ShapeDtypeStruct(estimate.shape, F32),
        in_specs=[some] * 4,
        out_specs=vmem,
        scratch_shapes=[
            pltpu.VMEM(estimate.shape, F32),
            pltpu.VMEM(images.shape, BF16),
            pltpu.VMEM((2 * hops + 1,) + line, BF16),
            pltpu.VMEM((views * rows, across + 2 * part, along), BF16),
            pltpu.VMEM((views * rows, across + 2 * part, along), BF16),
            pltpu.VMEM((views * rows, part, along), BF16),
            pltpu.VMEM((across, 3 * rows, along), F32),
            pltpu.VMEM((across, 3 * rows, along), I16),
            pltpu.VMEM((across, 3 * rows, along), I16),
        ]
        + [pltpu.VMEM(line, I16)] * 6
        + [
            pltpu.VMEM((4 * views, along), F32),
            pltpu.VMEM((views * rows, along), F32),
            pltpu.VMEM((views * rows, along), BF16),
            pltpu.VMEM(((2 * hops + 1) * rows, views * rows), BF16),
            pltpu.VMEM((views // 2, 2 * along, 2 * along), BF16),
            pltpu.VMEM((views // 2, 2 * along, 2 * along), BF16),
            pltpu.VMEM((views, part, across), BF16),
            pltpu.VMEM((views, part, across), BF16),
            pltpu.VMEM((across, along), F32),
            pltpu.VMEM((across, along), F32),
            pltpu.VMEM((3, views, tap_count), F32),
            pltpu.SMEM((views,), I32),
            pltpu.SemaphoreType.DMA((PARTS + 3,)),
            pltpu.SemaphoreType.DMA((6, PARTS)),
            pltpu.SemaphoreType.DMA((2 * hops + 1, PARTS)),
            pltpu.SemaphoreType.DMA((4, PARTS)),
            pltpu.SemaphoreType.DMA((4, PARTS)),
        ],
        compiler_params=pltpu.CompilerParams(
            collective_id=0, has_side_effects=True, vmem_limit_bytes=52 * 1024 * 1024
        ),
        name="restore",
    )(estimate, images, jnp.swapaxes(point_spread, 0, 1), shifts)
    return estimate * summed


def solution(mesh):
    in_specs = (
        P(("groups", "blocks"), None, None),
        P(None, ("groups", "blocks"), None, None),
        P(),
        P(),
    )
    out_specs = P(("groups", "blocks"), None, None)
    return jax.shard_map(body, mesh=mesh, in_specs=in_specs, out_specs=out_specs, check_vma=False)
```

```python
import functools

import jax
import jax.numpy as jnp
from jax import lax
from jax.experimental import pallas as pl
from jax.experimental.pallas import tpu as pltpu
from jax.sharding import PartitionSpec as P

SHIFT = 32
PARTS = 8
AHEAD = 6
FIRST = 2
MERGE, GATHER, FAR, FINISH = 4, 6, 4, 8
MAIN, HALT, STAY = 3, 9, 7
TOP = 4.2
F32 = jnp.float32
BF16 = jnp.bfloat16
I16 = jnp.int16
I32 = jnp.int32
MESH = pl.DeviceIdType.MESH


def dot(a, b):
    return jnp.dot(a, b, preferred_element_type=F32)


def coded(x):
    return ((x + 0.5).astype(I32) - 32768).astype(I16)


def decoded(q):
    return (q.astype(I32) + 32768).astype(F32)


def fused_kernel(
    dims,
    est_hbm,
    img_hbm,
    spread_hbm,
    shift_hbm,
    out_ref,
    est,
    img,
    win,
    held,
    ratio,
    back,
    own,
    mate_out,
    mate_in,
    far_out,
    far_in,
    on_out,
    on_in,
    dir_out,
    dir_in,
    taps,
    x_tmp,
    x_fwd,
    x_adj,
    z_fwd,
    z_adj,
    y_fwd,
    y_adj,
    scale,
    unscale,
    spread_ref,
    shift_ref,
    local_sem,
    send_sem,
    recv_sem,
    back_send,
    back_recv,
):
    count, views, rows, across, along, tap_count, hops = dims
    margin = tap_count // 2
    part = across // PARTS
    mid = hops
    slab = rows * count
    me = lax.axis_index("blocks")
    odd = lax.rem(me, 2)
    right = lax.rem(me, 4) // 2
    mate = 1 - 2 * odd
    far = -3 * mate
    side = 2 - 4 * right
    up = 2 - 2 * right
    down = 2 * right
    beyond = (me + 2 * side >= 0) & (me + 2 * side < count)
    before = (me - 2 * side >= 0) & (me - 2 * side < count)
    away = (me + far >= 0) & (me + far < count)

    barrier = pltpu.get_barrier_semaphore()

    def signal(there):
        pl.semaphore_signal(barrier, inc=1, device_id={"blocks": there}, device_id_type=MESH)

    signal(me + mate)
    signal(me + side)
    pl.when(beyond)(lambda: signal(me + 2 * side))
    pl.when(before)(lambda: signal(me - 2 * side))
    pl.when(away)(lambda: signal(me + far))

    def span(j):
        return pl.ds(pl.multiple_of(j * part, part), part)

    def load_est(j):
        return pltpu.make_async_copy(est_hbm.at[:, span(j)], est.at[:, span(j)], local_sem.at[j])

    load_img = pltpu.make_async_copy(img_hbm, img, local_sem.at[PARTS])

    @pl.loop(0, PARTS)
    def _(j):
        load_est(j).start()

    load_spread = pltpu.make_async_copy(spread_hbm, spread_ref, local_sem.at[PARTS + 1])
    load_shift = pltpu.make_async_copy(shift_hbm, shift_ref, local_sem.at[PARTS + 2])
    load_spread.start()
    load_shift.start()
    load_img.start()

    def send(from_slot, to_slot, there, kind, j):
        return pltpu.make_async_remote_copy(
            src_ref=win.at[from_slot, span(j)],
            dst_ref=win.at[to_slot, span(j)],
            send_sem=send_sem.at[kind, j],
            recv_sem=recv_sem.at[to_slot, j],
            device_id={"blocks": there},
            device_id_type=MESH,
        )

    def direct(j):
        return send(mid, mid - side, me + side, 0, j)

    def onward(j):
        return send(mid + side, mid - side, me + 2 * side, 1, j)

    def long(j):
        return send(mid, mid - far, me + far, 2, j)

    def near(j):
        return send(mid, mid - mate, me + mate, 3, j)

    def pass_near(j):
        return send(mid + side, mid + side - mate, me + mate, 4, j)

    def pass_back(j):
        return send(mid - side, mid - side - mate, me + mate, 5, j)

    def landed(offset, j):
        return send(mid, mid + offset, me + mate, 0, j)

    def prepare(j):
        load_est(j).wait()
        win[mid, span(j)] = jnp.swapaxes(est[:, span(j), :].astype(BF16), 0, 1)

    prepare(0)
    peers = 2 + beyond.astype(I32) + before.astype(I32) + away.astype(I32)
    pl.semaphore_wait(barrier, peers)

    @pl.loop(0, PARTS)
    def _(j):
        pl.when(j > 0)(lambda: prepare(j))
        direct(j).start()
        pl.when((j < FIRST) & away)(lambda: long(j).start())
        near(j).start()

    def build_across():
        for offset in range(-hops, hops + 1):
            there = me + offset
            if offset:

                @pl.when((there < 0) | (there >= count))
                def _():
                    win[mid + offset] = jnp.zeros(win.shape[1:], BF16)

        def none_in(ref):
            ref[...] = jnp.full(ref.shape, -32768, I16)

        for edge in (0, across + part):
            held[:, edge : edge + part] = jnp.zeros((views * rows, part, along), BF16)
            ratio[:, edge : edge + part] = jnp.zeros((views * rows, part, along), BF16)

        pl.when(jnp.logical_not(beyond))(lambda: none_in(on_in))
        pl.when(jnp.logical_not(away))(lambda: none_in(far_in))

        every = taps[...].astype(BF16)
        r = lax.broadcasted_iota(I32, (along, along), 0)
        c = lax.broadcasted_iota(I32, (along, along), 1)
        place = jnp.where(c < along // 2, c, c - along)
        plus = dot(every, (r == margin + place).astype(F32).astype(BF16))
        minus = dot(every, (r == margin - place).astype(F32).astype(BF16))
        close = jnp.abs(r - c) <= margin

        def turned(lines, row):
            line = jnp.broadcast_to(lines[row : row + 1], (along, along))
            return jnp.where(close, pltpu.roll(line, 0, 1, stride=1, stride_axis=0), 0.0)

        z_fwd[...] = jnp.zeros(z_fwd.shape, BF16)
        z_adj[...] = jnp.zeros(z_adj.shape, BF16)
        gains = [[], [], []]
        for v in range(views):
            half = pl.ds((v % 2) * along, along)
            for a in range(3):
                m = turned(minus, a * views + v)
                p = turned(plus, a * views + v).astype(BF16)
                inv = 1.0 / jnp.sum(m, axis=0, keepdims=True)
                gains[a].append(dot(jnp.broadcast_to(inv, (16, along)).astype(BF16), p)[:1])
                if a == 1:
                    y_fwd[v] = p[part : 2 * part]
                    y_adj[v] = m[part : 2 * part].astype(BF16)
                if a == 2:
                    z_fwd[v // 2, half, half] = m.astype(BF16)
                    z_adj[v // 2, half, half] = p
        gain_x, gain_y, gain_z = [jnp.concatenate(g, axis=0) for g in gains]
        left = gain_y * jnp.max(gain_x, axis=1, keepdims=True)
        bound = lax.dot_general(left, gain_z, (((0,), (0,)), ((), ())), preferred_element_type=F32)
        bound = bound * (TOP * 1.03)
        scale[...] = 65535.0 / bound
        unscale[...] = bound / (65535.0 * views)

    def build_rows():
        taps[...] = jnp.zeros(taps.shape, F32)
        for v in range(views):
            for a in range(3):
                line = spread_ref[a, pl.ds(v, 1), :]
                total = jnp.sum(line, axis=1, keepdims=True)
                taps[pl.ds(a * views + v, 1), pl.ds(0, tap_count)] = (line / total).astype(BF16).astype(F32)

        shifts = jnp.zeros((views, along), I32)
        v_of = lax.broadcasted_iota(I32, (views, along), 0)
        w_of = lax.broadcasted_iota(I32, (views, along), 1)
        for v in range(views):
            shifts = jnp.where(v_of == v, shift_ref[v], shifts)
        index = w_of + shifts + (margin - rows * hops)
        x_taps = taps[pl.ds(0, views), :]
        x_line = jnp.zeros((views, along), F32)
        for j in range(tap_count):
            x_line = jnp.where(index == j, jnp.broadcast_to(x_taps[:, j : j + 1], (views, along)), x_line)
        r_of = lax.broadcasted_iota(I32, (rows, along), 0)
        c_of = lax.broadcasted_iota(I32, (rows, along), 1)
        still = jnp.where(c_of == r_of + rows * hops, 1.0, 0.0)
        for v in range(views):
            line = jnp.broadcast_to(x_line[v : v + 1], (rows, along))
            x = pltpu.roll(line, 0, 1, stride=1, stride_axis=0)
            row = me * rows + r_of - jnp.broadcast_to(shifts[v : v + 1], (rows, along))
            valid = (row >= 0) & (row < slab)
            x_fwd[pl.ds(v * rows, rows), :] = jnp.where(valid, x, still).astype(BF16)
            x_tmp[pl.ds(v * rows, rows), :] = jnp.where(valid, x, 0.0)
        x_tmp[...] = jnp.transpose(x_tmp[...])

        def rows_of(block):
            return x_tmp[pl.ds(pl.multiple_of(block * rows, rows), rows), :].astype(BF16)

        for k in range(3):
            x_adj[pl.ds(k * rows, rows), :] = rows_of(2 * k + 1)
            x_adj[pl.ds((3 + k) * rows, rows), :] = rows_of(2 * k + 2 - 2 * odd)
        x_adj[pl.ds(6 * rows, rows), :] = rows_of(6 * odd)

    width = rows * (2 * hops + 1)

    def forward(j):
        base = pl.multiple_of(j * part, part)
        slabs = []
        for p in range(0, part, 2):
            pair = [win[:, base + p + q].reshape(width, along) for q in range(2)]
            res = dot(x_fwd[:, :width], jnp.concatenate(pair, axis=1)).astype(BF16)
            slabs += [res[:, :along], res[:, along:]]
        for w in range(views // 2):
            both = []
            for v in (2 * w, 2 * w + 1):
                both.append(jnp.concatenate([s[v * rows : (v + 1) * rows] for s in slabs], axis=0))
            res = dot(jnp.concatenate(both, axis=1), z_fwd[w]).astype(BF16)
            for q in range(2):
                block = res[:, q * along : (q + 1) * along].reshape(part, rows, along)
                there = pl.ds(pl.multiple_of(base + part, part), part)
                held[pl.ds((2 * w + q) * rows, rows), there, :] = jnp.swapaxes(block, 0, 1)

    def divide(j):
        out = pl.ds(pl.multiple_of((j + 1) * part, part), part)
        window = pl.ds(pl.multiple_of(j * part, part), 3 * part)
        for v in range(views):
            for i in range(0, rows, 2):
                pair = [held[v * rows + i + q, window] for q in range(2)]
                blurred = dot(y_fwd[v, :, : 3 * part], jnp.concatenate(pair, axis=1))
                image = jnp.concatenate([img[v, i + q, span(j)].astype(F32) for q in range(2)], axis=1)
                result = (image / blurred).astype(BF16)
                for q in range(2):
                    ratio[v * rows + i + q, out] = result[:, q * along : (q + 1) * along]

    def spread_back(j):
        window = pl.ds(pl.multiple_of(j * part, part), 3 * part)
        for v in range(views):
            for i in range(0, rows, 2):
                pair = [ratio[v * rows + i + q, window] for q in range(2)]
                res = dot(y_adj[v, :, : 3 * part], jnp.concatenate(pair, axis=1)).astype(BF16)
                for q in range(2):
                    back[v * rows + i + q] = res[:, q * along : (q + 1) * along]

    def back_send_copy(src, dst, there, kind, j):
        return pltpu.make_async_remote_copy(
            src_ref=src.at[span(j)],
            dst_ref=dst.at[span(j)],
            send_sem=back_send.at[kind, j],
            recv_sem=back_recv.at[kind, j],
            device_id={"blocks": there},
            device_id_type=MESH,
        )

    def to_mate(j):
        return back_send_copy(mate_out, mate_in, me + mate, 0, j)

    def to_far(j):
        return back_send_copy(far_out, far_in, me + far, 1, j)

    def to_on(j):
        return back_send_copy(on_out, on_in, me - 2 * side, 2, j)

    def to_side(j):
        return back_send_copy(dir_out, dir_in, me + side, 3, j)

    def backward(j):
        base = pl.multiple_of(j * part, part)
        cols = []
        for w in range(views // 2):
            both = [
                back[pl.ds((2 * w + q) * rows, rows)].reshape(rows * part, along)
                for q in range(2)
            ]
            res = dot(jnp.concatenate(both, axis=1), z_adj[w]).astype(BF16)
            for q in range(2):
                block = res[:, q * along : (q + 1) * along].reshape(rows, part, along)
                cols.append(jnp.swapaxes(block, 0, 1))
        for p in range(0, part, 2):
            pair = [jnp.concatenate([col[p + q] for col in cols], axis=0) for q in range(2)]
            both = dot(x_adj[...], jnp.concatenate(pair, axis=1))
            for q in range(2):
                y = base + p + q
                res = both[:, q * along : (q + 1) * along] * scale[pl.ds(y, 1), :]
                own[y] = res[: 3 * rows]
                mate_out[y] = coded(res[3 * rows : 6 * rows])
                far_out[y] = coded(res[6 * rows :])

    def merge(j):
        base = pl.multiple_of(j * part, part)
        own[pl.ds(base, part)] += decoded(mate_in[pl.ds(base, part)])
        pick = pl.ds(pl.multiple_of(down * rows, rows), rows)

        @pl.when(before)
        def _():
            on_out[pl.ds(base, part)] = coded(own[pl.ds(base, part), pick, :])

    def gather(j):
        base = pl.multiple_of(j * part, part)
        pick = pl.ds(pl.multiple_of(up * rows, rows), rows)
        total = own[pl.ds(base, part), pick, :] + decoded(on_in[pl.ds(base, part)])
        dir_out[pl.ds(base, part)] = coded(total)

    def finish(j):
        base = pl.multiple_of(j * part, part)
        there = pl.ds(base, part)
        total = own[there, pl.ds(rows, rows), :] + decoded(dir_in[there]) + decoded(far_in[there])
        out_ref[:, there, :] = jnp.swapaxes(total, 0, 1) * unscale[there, :]

    def combine(j):
        to_mate(j).wait_recv()
        merge(j)
        pl.when(before)(lambda: to_on(j).start())

    def collect(j):
        pl.when(beyond)(lambda: to_on(j).wait_recv())
        gather(j)
        to_side(j).start()

    def close(j):
        to_side(j).wait_recv()
        pl.when(away)(lambda: to_far(j).wait_recv())
        finish(j)

    def relay(j):
        landed(side, j).wait_recv()
        pl.when(beyond)(lambda: onward(j).start())
        pass_near(j).start()
        pl.when((j + FIRST < PARTS) & away)(lambda: long(j + FIRST).start())

    def ahead(t):
        return jnp.minimum(PARTS, (3 * t + AHEAD) // 2)

    load_spread.wait()
    load_shift.wait()
    build_rows()
    relay(0)
    build_across()

    @pl.loop(0, PARTS + MAIN)
    def _(t):
        def step(lag):
            j = t - lag
            return pl.when((j >= 0) & (j < PARTS)), j

        first = jnp.where(t == 0, 1, ahead(t - 1))
        pl.loop(first, jnp.maximum(first, ahead(t)))(relay)

        now, _ = step(0)

        @now
        def _():
            @pl.when(before)
            def _():
                landed(-side, t).wait_recv()
                pass_back(t).start()

        now, a = step(1)

        @now
        def _():
            landed(mate, a).wait_recv()
            landed(side + mate, a).wait_recv()
            pl.when(before)(lambda: landed(mate - side, a).wait_recv())
            pl.when(away)(lambda: landed(far, a).wait_recv())
            forward(a)

        pl.when(t == 2)(load_img.wait)
        now, b = step(2)
        now(lambda: divide(b))
        now, c = step(3)

        @now
        def _():
            spread_back(c)
            backward(c)
            to_mate(c).start()

        now, d = step(MERGE)

        now(lambda: combine(d))
        now, e = step(FAR)
        now(lambda: pl.when(away)(lambda: to_far(e).start()))
        now, f = step(GATHER)
        pl.when(t <= HALT)(lambda: now(lambda: collect(f)))
        now, g = step(FINISH)
        pl.when(t <= STAY)(lambda: now(lambda: close(g)))

    for d in range(PARTS + MAIN - MERGE, PARTS):
        combine(d)
    for e in range(PARTS + MAIN - FAR, PARTS):
        pl.when(away)(lambda: to_far(e).start())
    late = HALT - GATHER + 1
    done = max(0, STAY - FINISH + 1)

    @pl.loop(0, PARTS - done)
    def _(i):
        pl.when(i + late < PARTS)(lambda: collect(i + late))
        close(i + done)

    @pl.loop(0, PARTS)
    def _(j):
        direct(j).wait_send()
        near(j).wait_send()
        pass_near(j).wait_send()
        to_mate(j).wait_send()
        to_side(j).wait_send()

        @pl.when(away)
        def _():
            long(j).wait_send()
            to_far(j).wait_send()

        pl.when(beyond)(lambda: onward(j).wait_send())

        @pl.when(before)
        def _():
            pass_back(j).wait_send()
            to_on(j).wait_send()


def body(estimate, images, point_spread, shifts):
    views = images.shape[0]
    rows, across, along = estimate.shape
    tap_count = point_spread.shape[2]
    count = lax.axis_size("blocks")
    hops = -(-(tap_count // 2 + SHIFT) // rows)
    dims = (count, views, rows, across, along, tap_count, hops)
    some = pl.BlockSpec(memory_space=pltpu.HBM)
    vmem = pl.BlockSpec(memory_space=pltpu.VMEM)
    line = (across, rows, along)
    part = across // PARTS
    summed = pl.pallas_call(
        functools.partial(fused_kernel, dims),
        out_shape=jax.ShapeDtypeStruct(estimate.shape, F32),
        in_specs=[some] * 4,
        out_specs=vmem,
        scratch_shapes=[
            pltpu.VMEM(estimate.shape, F32),
            pltpu.VMEM(images.shape, BF16),
            pltpu.VMEM((2 * hops + 1,) + line, BF16),
            pltpu.VMEM((views * rows, across + 2 * part, along), BF16),
            pltpu.VMEM((views * rows, across + 2 * part, along), BF16),
            pltpu.VMEM((views * rows, part, along), BF16),
            pltpu.VMEM((across, 3 * rows, along), F32),
            pltpu.VMEM((across, 3 * rows, along), I16),
            pltpu.VMEM((across, 3 * rows, along), I16),
        ]
        + [pltpu.VMEM(line, I16)] * 6
        + [
            pltpu.VMEM((4 * views, along), F32),
            pltpu.VMEM((views * rows, along), F32),
            pltpu.VMEM((views * rows, along), BF16),
            pltpu.VMEM(((2 * hops + 1) * rows, views * rows), BF16),
            pltpu.VMEM((views // 2, 2 * along, 2 * along), BF16),
            pltpu.VMEM((views // 2, 2 * along, 2 * along), BF16),
            pltpu.VMEM((views, part, across), BF16),
            pltpu.VMEM((views, part, across), BF16),
            pltpu.VMEM((across, along), F32),
            pltpu.VMEM((across, along), F32),
            pltpu.VMEM((3, views, tap_count), F32),
            pltpu.SMEM((views,), I32),
            pltpu.SemaphoreType.DMA((PARTS + 3,)),
            pltpu.SemaphoreType.DMA((6, PARTS)),
            pltpu.SemaphoreType.DMA((2 * hops + 1, PARTS)),
            pltpu.SemaphoreType.DMA((4, PARTS)),
            pltpu.SemaphoreType.DMA((4, PARTS)),
        ],
        compiler_params=pltpu.CompilerParams(
            collective_id=0, has_side_effects=True, vmem_limit_bytes=52 * 1024 * 1024
        ),
        name="restore",
    )(estimate, images, jnp.swapaxes(point_spread, 0, 1), shifts)
    return estimate * summed


def solution(mesh):
    in_specs = (
        P(("groups", "blocks"), None, None),
        P(None, ("groups", "blocks"), None, None),
        P(),
        P(),
    )
    out_specs = P(("groups", "blocks"), None, None)
    return jax.shard_map(body, mesh=mesh, in_specs=in_specs, out_specs=out_specs, check_vma=False)
```

```python
import functools

import jax
import jax.numpy as jnp
from jax import lax
from jax.experimental import pallas as pl
from jax.experimental.pallas import tpu as pltpu
from jax.sharding import PartitionSpec as P

SHIFT = 32
PARTS = 8
AHEAD = 6
FIRST = 2
MERGE, GATHER, FAR, FINISH = 4, 6, 6, 8
MAIN, HALT, STAY = 3, 10, 7
TOP = 4.2
F32 = jnp.float32
BF16 = jnp.bfloat16
I16 = jnp.int16
I32 = jnp.int32
MESH = pl.DeviceIdType.MESH


def dot(a, b):
    return jnp.dot(a, b, preferred_element_type=F32)


def coded(x):
    return ((x + 0.5).astype(I32) - 32768).astype(I16)


def decoded(q):
    return (q.astype(I32) + 32768).astype(F32)


def fused_kernel(
    dims,
    est_hbm,
    img_hbm,
    spread_hbm,
    shift_hbm,
    out_ref,
    est,
    img,
    win,
    held,
    ratio,
    back,
    own,
    mate_out,
    mate_in,
    far_out,
    far_in,
    on_out,
    on_in,
    dir_out,
    dir_in,
    taps,
    x_tmp,
    x_fwd,
    x_adj,
    z_fwd,
    z_adj,
    y_fwd,
    y_adj,
    scale,
    unscale,
    spread_ref,
    shift_ref,
    local_sem,
    send_sem,
    recv_sem,
    back_send,
    back_recv,
):
    count, views, rows, across, along, tap_count, hops = dims
    margin = tap_count // 2
    part = across // PARTS
    mid = hops
    slab = rows * count
    me = lax.axis_index("blocks")
    odd = lax.rem(me, 2)
    right = lax.rem(me, 4) // 2
    mate = 1 - 2 * odd
    far = -3 * mate
    side = 2 - 4 * right
    up = 2 - 2 * right
    down = 2 * right
    beyond = (me + 2 * side >= 0) & (me + 2 * side < count)
    before = (me - 2 * side >= 0) & (me - 2 * side < count)
    away = (me + far >= 0) & (me + far < count)

    barrier = pltpu.get_barrier_semaphore()

    def signal(there):
        pl.semaphore_signal(barrier, inc=1, device_id={"blocks": there}, device_id_type=MESH)

    signal(me + mate)
    signal(me + side)
    pl.when(beyond)(lambda: signal(me + 2 * side))
    pl.when(before)(lambda: signal(me - 2 * side))
    pl.when(away)(lambda: signal(me + far))

    def span(j):
        return pl.ds(pl.multiple_of(j * part, part), part)

    def load_est(j):
        return pltpu.make_async_copy(est_hbm.at[:, span(j)], est.at[:, span(j)], local_sem.at[j])

    load_img = pltpu.make_async_copy(img_hbm, img, local_sem.at[PARTS])

    @pl.loop(0, PARTS)
    def _(j):
        load_est(j).start()

    load_spread = pltpu.make_async_copy(spread_hbm, spread_ref, local_sem.at[PARTS + 1])
    load_shift = pltpu.make_async_copy(shift_hbm, shift_ref, local_sem.at[PARTS + 2])
    load_spread.start()
    load_shift.start()
    load_img.start()

    def send(from_slot, to_slot, there, kind, j):
        return pltpu.make_async_remote_copy(
            src_ref=win.at[from_slot, span(j)],
            dst_ref=win.at[to_slot, span(j)],
            send_sem=send_sem.at[kind, j],
            recv_sem=recv_sem.at[to_slot, j],
            device_id={"blocks": there},
            device_id_type=MESH,
        )

    def direct(j):
        return send(mid, mid - side, me + side, 0, j)

    def onward(j):
        return send(mid + side, mid - side, me + 2 * side, 1, j)

    def long(j):
        return send(mid, mid - far, me + far, 2, j)

    def near(j):
        return send(mid, mid - mate, me + mate, 3, j)

    def pass_near(j):
        return send(mid + side, mid + side - mate, me + mate, 4, j)

    def pass_back(j):
        return send(mid - side, mid - side - mate, me + mate, 5, j)

    def landed(offset, j):
        return send(mid, mid + offset, me + mate, 0, j)

    def prepare(j):
        load_est(j).wait()
        win[mid, span(j)] = jnp.swapaxes(est[:, span(j), :].astype(BF16), 0, 1)

    prepare(0)
    peers = 2 + beyond.astype(I32) + before.astype(I32) + away.astype(I32)
    pl.semaphore_wait(barrier, peers)

    @pl.loop(0, PARTS)
    def _(j):
        pl.when(j > 0)(lambda: prepare(j))
        direct(j).start()
        pl.when((j < FIRST) & away)(lambda: long(j).start())
        near(j).start()

    def build_across():
        for offset in range(-hops, hops + 1):
            there = me + offset
            if offset:

                @pl.when((there < 0) | (there >= count))
                def _():
                    win[mid + offset] = jnp.zeros(win.shape[1:], BF16)

        def none_in(ref):
            ref[...] = jnp.full(ref.shape, -32768, I16)

        for edge in (0, across + part):
            held[:, edge : edge + part] = jnp.zeros((views * rows, part, along), BF16)
            ratio[:, edge : edge + part] = jnp.zeros((views * rows, part, along), BF16)

        pl.when(jnp.logical_not(beyond))(lambda: none_in(on_in))
        pl.when(jnp.logical_not(away))(lambda: none_in(far_in))

        every = taps[...].astype(BF16)
        r = lax.broadcasted_iota(I32, (along, along), 0)
        c = lax.broadcasted_iota(I32, (along, along), 1)
        place = jnp.where(c < along // 2, c, c - along)
        plus = dot(every, (r == margin + place).astype(F32).astype(BF16))
        minus = dot(every, (r == margin - place).astype(F32).astype(BF16))
        close = jnp.abs(r - c) <= margin

        def turned(lines, row):
            line = jnp.broadcast_to(lines[row : row + 1], (along, along))
            return jnp.where(close, pltpu.roll(line, 0, 1, stride=1, stride_axis=0), 0.0)

        z_fwd[...] = jnp.zeros(z_fwd.shape, BF16)
        z_adj[...] = jnp.zeros(z_adj.shape, BF16)
        gains = [[], [], []]
        for v in range(views):
            half = pl.ds((v % 2) * along, along)
            for a in range(3):
                m = turned(minus, a * views + v)
                p = turned(plus, a * views + v).astype(BF16)
                inv = 1.0 / jnp.sum(m, axis=0, keepdims=True)
                gains[a].append(dot(jnp.broadcast_to(inv, (16, along)).astype(BF16), p)[:1])
                if a == 1:
                    y_fwd[v] = p[part : 2 * part]
                    y_adj[v] = m[part : 2 * part].astype(BF16)
                if a == 2:
                    z_fwd[v // 2, half, half] = m.astype(BF16)
                    z_adj[v // 2, half, half] = p
        gain_x, gain_y, gain_z = [jnp.concatenate(g, axis=0) for g in gains]
        left = gain_y * jnp.max(gain_x, axis=1, keepdims=True)
        bound = lax.dot_general(left, gain_z, (((0,), (0,)), ((), ())), preferred_element_type=F32)
        bound = bound * (TOP * 1.03)
        scale[...] = 65535.0 / bound
        unscale[...] = bound / (65535.0 * views)

    def build_rows():
        taps[...] = jnp.zeros(taps.shape, F32)
        for v in range(views):
            for a in range(3):
                line = spread_ref[a, pl.ds(v, 1), :]
                total = jnp.sum(line, axis=1, keepdims=True)
                taps[pl.ds(a * views + v, 1), pl.ds(0, tap_count)] = (line / total).astype(BF16).astype(F32)

        shifts = jnp.zeros((views, along), I32)
        v_of = lax.broadcasted_iota(I32, (views, along), 0)
        w_of = lax.broadcasted_iota(I32, (views, along), 1)
        for v in range(views):
            shifts = jnp.where(v_of == v, shift_ref[v], shifts)
        index = w_of + shifts + (margin - rows * hops)
        x_taps = taps[pl.ds(0, views), :]
        x_line = jnp.zeros((views, along), F32)
        for j in range(tap_count):
            x_line = jnp.where(index == j, jnp.broadcast_to(x_taps[:, j : j + 1], (views, along)), x_line)
        r_of = lax.broadcasted_iota(I32, (rows, along), 0)
        c_of = lax.broadcasted_iota(I32, (rows, along), 1)
        still = jnp.where(c_of == r_of + rows * hops, 1.0, 0.0)
        for v in range(views):
            line = jnp.broadcast_to(x_line[v : v + 1], (rows, along))
            x = pltpu.roll(line, 0, 1, stride=1, stride_axis=0)
            row = me * rows + r_of - jnp.broadcast_to(shifts[v : v + 1], (rows, along))
            valid = (row >= 0) & (row < slab)
            x_fwd[pl.ds(v * rows, rows), :] = jnp.where(valid, x, still).astype(BF16)
            x_tmp[pl.ds(v * rows, rows), :] = jnp.where(valid, x, 0.0)
        x_tmp[...] = jnp.transpose(x_tmp[...])

        def rows_of(block):
            return x_tmp[pl.ds(pl.multiple_of(block * rows, rows), rows), :].astype(BF16)

        for k in range(3):
            x_adj[pl.ds(k * rows, rows), :] = rows_of(2 * k + 1)
            x_adj[pl.ds((3 + k) * rows, rows), :] = rows_of(2 * k + 2 - 2 * odd)
        x_adj[pl.ds(6 * rows, rows), :] = rows_of(6 * odd)

    width = rows * (2 * hops + 1)

    def forward(j):
        base = pl.multiple_of(j * part, part)
        slabs = []
        for p in range(0, part, 2):
            pair = [win[:, base + p + q].reshape(width, along) for q in range(2)]
            res = dot(x_fwd[:, :width], jnp.concatenate(pair, axis=1)).astype(BF16)
            slabs += [res[:, :along], res[:, along:]]
        for w in range(views // 2):
            both = []
            for v in (2 * w, 2 * w + 1):
                both.append(jnp.concatenate([s[v * rows : (v + 1) * rows] for s in slabs], axis=0))
            res = dot(jnp.concatenate(both, axis=1), z_fwd[w]).astype(BF16)
            for q in range(2):
                block = res[:, q * along : (q + 1) * along].reshape(part, rows, along)
                there = pl.ds(pl.multiple_of(base + part, part), part)
                held[pl.ds((2 * w + q) * rows, rows), there, :] = jnp.swapaxes(block, 0, 1)

    def divide(j):
        out = pl.ds(pl.multiple_of((j + 1) * part, part), part)
        window = pl.ds(pl.multiple_of(j * part, part), 3 * part)
        for v in range(views):
            for i in range(0, rows, 2):
                pair = [held[v * rows + i + q, window] for q in range(2)]
                blurred = dot(y_fwd[v, :, : 3 * part], jnp.concatenate(pair, axis=1))
                image = jnp.concatenate([img[v, i + q, span(j)].astype(F32) for q in range(2)], axis=1)
                result = (image / blurred).astype(BF16)
                for q in range(2):
                    ratio[v * rows + i + q, out] = result[:, q * along : (q + 1) * along]

    def spread_back(j):
        window = pl.ds(pl.multiple_of(j * part, part), 3 * part)
        for v in range(views):
            for i in range(0, rows, 2):
                pair = [ratio[v * rows + i + q, window] for q in range(2)]
                res = dot(y_adj[v, :, : 3 * part], jnp.concatenate(pair, axis=1)).astype(BF16)
                for q in range(2):
                    back[v * rows + i + q] = res[:, q * along : (q + 1) * along]

    def back_send_copy(src, dst, there, kind, j):
        return pltpu.make_async_remote_copy(
            src_ref=src.at[span(j)],
            dst_ref=dst.at[span(j)],
            send_sem=back_send.at[kind, j],
            recv_sem=back_recv.at[kind, j],
            device_id={"blocks": there},
            device_id_type=MESH,
        )

    def to_mate(j):
        return back_send_copy(mate_out, mate_in, me + mate, 0, j)

    def to_far(j):
        return back_send_copy(far_out, far_in, me + far, 1, j)

    def to_on(j):
        return back_send_copy(on_out, on_in, me - 2 * side, 2, j)

    def to_side(j):
        return back_send_copy(dir_out, dir_in, me + side, 3, j)

    def backward(j):
        base = pl.multiple_of(j * part, part)
        cols = []
        for w in range(views // 2):
            both = [
                back[pl.ds((2 * w + q) * rows, rows)].reshape(rows * part, along)
                for q in range(2)
            ]
            res = dot(jnp.concatenate(both, axis=1), z_adj[w]).astype(BF16)
            for q in range(2):
                block = res[:, q * along : (q + 1) * along].reshape(rows, part, along)
                cols.append(jnp.swapaxes(block, 0, 1))
        for p in range(0, part, 2):
            pair = [jnp.concatenate([col[p + q] for col in cols], axis=0) for q in range(2)]
            both = dot(x_adj[...], jnp.concatenate(pair, axis=1))
            for q in range(2):
                y = base + p + q
                res = both[:, q * along : (q + 1) * along] * scale[pl.ds(y, 1), :]
                own[y] = res[: 3 * rows]
                mate_out[y] = coded(res[3 * rows : 6 * rows])
                far_out[y] = coded(res[6 * rows :])

    def merge(j):
        base = pl.multiple_of(j * part, part)
        own[pl.ds(base, part)] += decoded(mate_in[pl.ds(base, part)])
        pick = pl.ds(pl.multiple_of(down * rows, rows), rows)

        @pl.when(before)
        def _():
            on_out[pl.ds(base, part)] = coded(own[pl.ds(base, part), pick, :])

    def gather(j):
        base = pl.multiple_of(j * part, part)
        pick = pl.ds(pl.multiple_of(up * rows, rows), rows)
        total = own[pl.ds(base, part), pick, :] + decoded(on_in[pl.ds(base, part)])
        dir_out[pl.ds(base, part)] = coded(total)

    def finish(j):
        base = pl.multiple_of(j * part, part)
        there = pl.ds(base, part)
        total = own[there, pl.ds(rows, rows), :] + decoded(dir_in[there]) + decoded(far_in[there])
        out_ref[:, there, :] = jnp.swapaxes(total, 0, 1) * unscale[there, :]

    def combine(j):
        to_mate(j).wait_recv()
        merge(j)
        pl.when(before)(lambda: to_on(j).start())

    def collect(j):
        pl.when(beyond)(lambda: to_on(j).wait_recv())
        gather(j)
        to_side(j).start()

    def close(j):
        to_side(j).wait_recv()
        pl.when(away)(lambda: to_far(j).wait_recv())
        finish(j)

    def relay(j):
        landed(side, j).wait_recv()
        pl.when(beyond)(lambda: onward(j).start())
        pass_near(j).start()
        pl.when((j + FIRST < PARTS) & away)(lambda: long(j + FIRST).start())

    def ahead(t):
        return jnp.minimum(PARTS, (3 * t + AHEAD) // 2)

    load_spread.wait()
    load_shift.wait()
    build_rows()
    relay(0)
    build_across()

    @pl.loop(0, PARTS + MAIN)
    def _(t):
        def step(lag):
            j = t - lag
            return pl.when((j >= 0) & (j < PARTS)), j

        first = jnp.where(t == 0, 1, ahead(t - 1))
        pl.loop(first, jnp.maximum(first, ahead(t)))(relay)

        now, _ = step(0)

        @now
        def _():
            @pl.when(before)
            def _():
                landed(-side, t).wait_recv()
                pass_back(t).start()

        now, a = step(1)

        @now
        def _():
            landed(mate, a).wait_recv()
            landed(side + mate, a).wait_recv()
            pl.when(before)(lambda: landed(mate - side, a).wait_recv())
            pl.when(away)(lambda: landed(far, a).wait_recv())
            forward(a)

        pl.when(t == 2)(load_img.wait)
        now, b = step(2)
        now(lambda: divide(b))
        now, c = step(3)

        @now
        def _():
            spread_back(c)
            backward(c)
            to_mate(c).start()

        now, d = step(MERGE)

        now(lambda: combine(d))
        now, e = step(FAR)
        now(lambda: pl.when(away)(lambda: to_far(e).start()))
        now, f = step(GATHER)
        pl.when(t <= HALT)(lambda: now(lambda: collect(f)))
        now, g = step(FINISH)
        pl.when(t <= STAY)(lambda: now(lambda: close(g)))

    for d in range(PARTS + MAIN - MERGE, PARTS):
        combine(d)
    for e in range(PARTS + MAIN - FAR, PARTS):
        pl.when(away)(lambda: to_far(e).start())
    late = HALT - GATHER + 1
    done = max(0, STAY - FINISH + 1)

    @pl.loop(0, PARTS - done)
    def _(i):
        pl.when(i + late < PARTS)(lambda: collect(i + late))
        close(i + done)

    @pl.loop(0, PARTS)
    def _(j):
        direct(j).wait_send()
        near(j).wait_send()
        pass_near(j).wait_send()
        to_mate(j).wait_send()
        to_side(j).wait_send()

        @pl.when(away)
        def _():
            long(j).wait_send()
            to_far(j).wait_send()

        pl.when(beyond)(lambda: onward(j).wait_send())

        @pl.when(before)
        def _():
            pass_back(j).wait_send()
            to_on(j).wait_send()


def body(estimate, images, point_spread, shifts):
    views = images.shape[0]
    rows, across, along = estimate.shape
    tap_count = point_spread.shape[2]
    count = lax.axis_size("blocks")
    hops = -(-(tap_count // 2 + SHIFT) // rows)
    dims = (count, views, rows, across, along, tap_count, hops)
    some = pl.BlockSpec(memory_space=pltpu.HBM)
    vmem = pl.BlockSpec(memory_space=pltpu.VMEM)
    line = (across, rows, along)
    part = across // PARTS
    summed = pl.pallas_call(
        functools.partial(fused_kernel, dims),
        out_shape=jax.ShapeDtypeStruct(estimate.shape, F32),
        in_specs=[some] * 4,
        out_specs=vmem,
        scratch_shapes=[
            pltpu.VMEM(estimate.shape, F32),
            pltpu.VMEM(images.shape, BF16),
            pltpu.VMEM((2 * hops + 1,) + line, BF16),
            pltpu.VMEM((views * rows, across + 2 * part, along), BF16),
            pltpu.VMEM((views * rows, across + 2 * part, along), BF16),
            pltpu.VMEM((views * rows, part, along), BF16),
            pltpu.VMEM((across, 3 * rows, along), F32),
            pltpu.VMEM((across, 3 * rows, along), I16),
            pltpu.VMEM((across, 3 * rows, along), I16),
        ]
        + [pltpu.VMEM(line, I16)] * 6
        + [
            pltpu.VMEM((4 * views, along), F32),
            pltpu.VMEM((views * rows, along), F32),
            pltpu.VMEM((views * rows, along), BF16),
            pltpu.VMEM(((2 * hops + 1) * rows, views * rows), BF16),
            pltpu.VMEM((views // 2, 2 * along, 2 * along), BF16),
            pltpu.VMEM((views // 2, 2 * along, 2 * along), BF16),
            pltpu.VMEM((views, part, across), BF16),
            pltpu.VMEM((views, part, across), BF16),
            pltpu.VMEM((across, along), F32),
            pltpu.VMEM((across, along), F32),
            pltpu.VMEM((3, views, tap_count), F32),
            pltpu.SMEM((views,), I32),
            pltpu.SemaphoreType.DMA((PARTS + 3,)),
            pltpu.SemaphoreType.DMA((6, PARTS)),
            pltpu.SemaphoreType.DMA((2 * hops + 1, PARTS)),
            pltpu.SemaphoreType.DMA((4, PARTS)),
            pltpu.SemaphoreType.DMA((4, PARTS)),
        ],
        compiler_params=pltpu.CompilerParams(
            collective_id=0, has_side_effects=True, vmem_limit_bytes=52 * 1024 * 1024
        ),
        name="restore",
    )(estimate, images, jnp.swapaxes(point_spread, 0, 1), shifts)
    return estimate * summed


def solution(mesh):
    in_specs = (
        P(("groups", "blocks"), None, None),
        P(None, ("groups", "blocks"), None, None),
        P(),
        P(),
    )
    out_specs = P(("groups", "blocks"), None, None)
    return jax.shard_map(body, mesh=mesh, in_specs=in_specs, out_specs=out_specs, check_vma=False)
```
